32 devices in a mesh: wa: 8 (over y, x, core), vert: 4 (over z).
Axes of the slice: x: 2, y: 2, z: 4, core: 2. Of those that a mesh axis runs over, the one named last changes fastest.
Arguments:
- spectra: bfloat16 [640, 2, 8, 1288], P('wa', None, 'vert'), may hold values from -0.4375 to 0.4375
- legendre: bfloat16 [640, 1288, 32], P('wa'), may hold values from -0.15625 to 0.15625
- pair_waves: int32 [640], replicated, may hold values from 0 to 639, each once
- points: int32 [64], P('wa'), may hold values from 20 to 5136, as said below
Outputs:
- gridded: float32 [64, 8, 5152], P('wa', None, 'vert')
The draws below stay inside these ranges and needn't reach their ends.
Inputs may be any that keep to these rules, and one draw needn't show every extreme that they name: Pair slot p holds wavenumbers pair_waves[p] and 1279 - pair_waves[p]; every value of 0 to 639 appears once. Each count is 20 plus four times a whole number; latitude 64 - 1 - i has as many points as latitude i.
All inputs are finite; a program needn't handle non-finite values.
Results may differ from the reference program's by a relative error of at most 0.0037.
Values may be sent and summed in bfloat16 or wider, within the bound.
A program may use at most 128 MiB of HBM per device.

```python
import math
import jax
import jax.numpy as jnp
from jax import lax

M = 1280
NPAIRS = 640
KPAD = 1288
NLAT = 64
NH = 32
FALL = 8
PTS = 5152


def draw_points(key, part):
    chosen = jax.random.randint(key, (NH,), 0, M)
    position = jax.random.randint(jax.random.fold_in(key, 7), (), 0, NH)
    chosen = jnp.where(jnp.arange(NH) == position, M - 1, chosen)
    northern = 20 + 4 * chosen
    return jnp.concatenate([northern, jnp.flip(northern)]).astype(jnp.int32)


def shard_levels(rng, dims, pieces, least, top_value):
    gain, own = 1.0, jax.random.fold_in(rng, 6)
    for axis_at, shards_of in pieces:
        draws = jnp.exp(jax.random.uniform(jax.random.fold_in(own, axis_at), (shards_of,), jnp.float32, least / len(pieces), top_value / len(pieces)))
        gain = gain * jnp.repeat(draws, dims[axis_at] // shards_of).reshape([-1 if axis == axis_at else 1 for axis in range(len(dims))])
    return gain


def centred(key, extent, deviation, limit, pieces=(), kind=jnp.bfloat16):
    values = jax.random.normal(key, extent, jnp.float32) * deviation
    if len(pieces) > 0:
        values = shard_levels(key, extent, pieces, -0.22, 0.18) * values
    return jnp.clip(values, min=-limit, max=limit).astype(kind)


def setup_inputs(seed: int = 0) -> dict:
    streams_of = jax.random.split(jax.random.key(seed), 5)
    spectra = centred(streams_of[0], (NPAIRS, 2, FALL, KPAD), (M ** -0.5), 0.4375, ((0, 8), (2, 4)))
    legendre = centred(streams_of[1], (NPAIRS, KPAD, NH), M ** -0.5, 0.15625, ((0, 8),))
    pair_waves = jax.random.permutation(streams_of[2], NPAIRS).astype(jnp.int32)
    points = draw_points(jax.random.fold_in(streams_of[4], 71), 0)
    return {"spectra": spectra, "legendre": legendre, "pair_waves": pair_waves, "points": points}


def legendre_selectors(lower_wavenumber_block, padded_length):
    column_index = jnp.arange(padded_length, dtype=jnp.int32)[None, :]
    boundary = M - lower_wavenumber_block[:, None]
    first_part = (column_index < boundary).astype(jnp.float32)
    second_part = ((column_index >= boundary) & (column_index < M + 1)).astype(jnp.float32)
    first_sign = jnp.where(column_index % 2 == 0, 1.0, -1.0).astype(jnp.float32)
    second_sign = jnp.where((column_index - boundary) % 2 == 0, 1.0, -1.0).astype(jnp.float32)
    return jnp.stack([first_part, first_part * first_sign, second_part, second_part * second_sign], axis=1)


def synthesis_tables(wave_numbers, length, point_index):
    phases = (wave_numbers[:, None] * point_index[None, :]) % length
    angles = phases.astype(jnp.float32) * (2.0 * math.pi) / length.astype(jnp.float32)
    weight = jnp.where(wave_numbers == 0, 1.0, jnp.where(2 * wave_numbers < length, 2.0, 0.0)).astype(jnp.float32)[:, None]
    cosine_basis = (weight * jnp.cos(angles)).astype(jnp.bfloat16)
    sine_part = (-(weight * jnp.sin(angles))).astype(jnp.bfloat16)
    return jnp.stack([cosine_basis, sine_part])


def reference(spectra, legendre, pair_waves, points):
    selectors = legendre_selectors(pair_waves, KPAD)

    def pair_project(input_arrays):
        spectrum, legendre_rows, selector = input_arrays
        masked = selector[:, None, None, :] * spectrum.astype(jnp.float32)[None]
        return jnp.einsum("qrfk,kh->qrfh", masked, legendre_rows.astype(jnp.float32))

    projected = lax.map(pair_project, (spectra, legendre, selectors))
    northern = projected[:, 0::2]
    southern = jnp.flip(projected[:, 1::2], -1)
    combined = jnp.concatenate([northern, southern], -1)
    fourier = combined.reshape(M, 2, FALL, NLAT).astype(jnp.bfloat16)
    wave_numbers = jnp.stack([pair_waves, M - 1 - pair_waves], axis=1).reshape(M)
    point_index = jnp.arange(PTS, dtype=jnp.int32)
    lat_first = jnp.moveaxis(fourier, 3, 0)

    def latitude_synthesis(input_arrays):
        spectral_weights, length = input_arrays
        basis_tables = synthesis_tables(wave_numbers, length, point_index)
        output_values = jnp.einsum("xnc,nxz->cz", spectral_weights.astype(jnp.float32), basis_tables.astype(jnp.float32))
        return jnp.where(point_index[None, :] < length, output_values, 0.0).astype(jnp.float32)

    return lax.map(latitude_synthesis, (lat_first, points))
```

```python
import functools
import math

import jax
import jax.numpy as jnp
from jax import lax
from jax.experimental import pallas as pl
from jax.experimental.pallas import tpu as pltpu
from jax.sharding import PartitionSpec as P

M = 1280
LANES = 128
SIN_PI = (
    math.pi,
    -math.pi**3 / 6,
    math.pi**5 / 120,
    -math.pi**7 / 5040,
    math.pi**9 / 362880,
    -math.pi**11 / 39916800,
    math.pi**13 / 6227020800,
)

COS_PI = (
    1.0,
    -math.pi**2 / 2,
    math.pi**4 / 24,
    -math.pi**6 / 720,
    math.pi**8 / 40320,
    -math.pi**10 / 3628800,
    math.pi**12 / 479001600,
)


def legendre_kernel(pair_block, bounds_ref, spectra_ref, legendre_ref, out_ref, scratch):
    step = pl.program_id(0)
    parts, fields, padded = spectra_ref.shape[1:]
    half = parts * fields
    heights = legendre_ref.shape[1]
    shape = (2 * half, padded)
    column = lax.broadcasted_iota(jnp.int32, shape, 1)
    plain = lax.broadcasted_iota(jnp.int32, shape, 0) < half
    alternating = jnp.where(plain | (column % 2 == 0), 1.0, -1.0)
    for i in range(pair_block):
        pair = step * pair_block + i
        boundary = M - bounds_ref[pair]
        flip = jnp.where(boundary % 2 == 0, 1.0, -1.0)
        rows = [spectra_ref[i, part].astype(jnp.float32) for part in range(parts)]
        signed = jnp.concatenate(rows + rows, axis=0) * alternating
        first = jnp.where(column < boundary, signed, 0.0)
        second = jnp.where((column >= boundary) & (column < M + 1), signed, 0.0)
        second = second * jnp.where(plain, 1.0, flip)
        masked = jnp.concatenate([first, second], axis=0).astype(jnp.bfloat16)
        scratch[pair, :, 0:heights] = lax.dot_general(
            masked,
            legendre_ref[i],
            (((1,), (1,)), ((), ())),
            preferred_element_type=jnp.float32,
        )

    @pl.when(step == pl.num_programs(0) - 1)
    def _():
        pairs = scratch.shape[0]
        blocks, _, lats, _ = out_ref.shape
        for sign in range(2):
            for row in range(half):
                halves = []
                for part in range(2):
                    picked = scratch[:, (part * 2 + sign) * half + row, :]
                    halves.append(jnp.transpose(picked)[:heights])
                both = jnp.concatenate(halves, axis=1).astype(jnp.bfloat16)
                for b in range(blocks // 2):
                    target = b if sign == 0 else blocks - 1 - b
                    out_ref[target, row] = both[b * lats : (b + 1) * lats]


def legendre_step(spectra, legendre, bounds, blocks):
    pairs, parts, fields, padded = spectra.shape
    heights = legendre.shape[1]
    block = 8 if pairs % 8 == 0 else 4
    lats = 2 * heights // blocks
    return pl.pallas_call(
        functools.partial(legendre_kernel, block),
        out_shape=jax.ShapeDtypeStruct((blocks, parts * fields, lats, 2 * pairs), jnp.bfloat16),
        grid=(pairs // block,),
        in_specs=[
            pl.BlockSpec(memory_space=pltpu.SMEM),
            pl.BlockSpec((block, parts, fields, padded), lambda i: (i, 0, 0, 0)),
            pl.BlockSpec((block, heights, padded), lambda i: (i, 0, 0)),
        ],
        out_specs=pl.BlockSpec((blocks, parts * fields, lats, 2 * pairs), lambda i: (0, 0, 0, 0)),
        scratch_shapes=[
            pltpu.VMEM((pairs, 4 * parts * fields, max(heights, LANES)), jnp.float32)
        ],
        name="legendre",
    )(bounds, spectra, legendre)


def trig(wave, offset, length, inverse):
    product = wave * offset
    turns = (product - jnp.round(product * inverse) * length) * inverse
    square = turns * turns
    sine = jnp.float32(SIN_PI[-1])
    for term in SIN_PI[-2::-1]:
        sine = sine * square + term
    sine = sine * turns
    cosine = jnp.float32(COS_PI[-1])
    for term in COS_PI[-2::-1]:
        cosine = cosine * square + term
    return 1.0 - 2.0 * sine * sine, 2.0 * sine * cosine


def gather_rows(arrived, fields_ref):
    columns, blocks, groups, lats, waves = arrived.shape
    half = groups // 2
    for v in range(columns):
        for g in range(groups):
            pieces = [arrived[v, w, g].astype(jnp.float32) for w in range(blocks)]
            fields_ref[:, g // half, v * half + g % half, :] = jnp.concatenate(pieces, axis=1)


def tables_of(wave, length, inverse, table_ref):
    row = lax.broadcasted_iota(jnp.int32, (8, 1), 0).astype(jnp.float32)
    fine_cos, fine_sin = trig(wave, row, length, inverse)
    for top in range(LANES // 64):
        coarse_cos, coarse_sin = trig(wave, 64 * top + 8 * row, length, inverse)
        for pair in range(4):
            cosines, sines = [], []
            for a in (2 * pair, 2 * pair + 1):
                c, s = coarse_cos[a : a + 1], coarse_sin[a : a + 1]
                cosines.append(c * fine_cos - s * fine_sin)
                sines.append(-(s * fine_cos + c * fine_sin))
            at = 64 * top + 16 * pair
            table_ref[at : at + 16, 0:M] = jnp.concatenate(cosines, axis=0).astype(jnp.bfloat16)
            table_ref[at : at + 16, M : 2 * M] = jnp.concatenate(sines, axis=0).astype(jnp.bfloat16)


def synthesis(wave, count, first_point, fields_ref, table_ref, left_ref, out_ref):
    length = count.astype(jnp.float32)
    inverse = 1.0 / length
    tables_of(wave, length, inverse, table_ref)
    fields, points = out_ref.shape
    weight = jnp.where(wave == 0, 1.0, jnp.where(2 * wave < length, 2.0, 0.0))
    row = lax.broadcasted_iota(jnp.int32, (8, 1), 0).astype(jnp.float32)
    start = first_point.astype(jnp.float32)
    blocks = pl.cdiv(points, LANES)
    for block in range(blocks):
        if block % 8 == 0:
            block_cos, block_sin = trig(wave, start + LANES * (block + row), length, inverse)
            block_cos, block_sin = block_cos * weight, block_sin * weight
        c = block_cos[block % 8 : block % 8 + 1]
        s = block_sin[block % 8 : block % 8 + 1]
        real, imag = fields_ref[0], fields_ref[1]
        at = block * fields
        left_ref[at : at + fields, 0:M] = (real * c - imag * s).astype(jnp.bfloat16)
        left_ref[at : at + fields, M : 2 * M] = (real * s + imag * c).astype(jnp.bfloat16)
    product = lax.dot_general(
        left_ref[...],
        table_ref[...],
        (((1,), (1,)), ((), ())),
        preferred_element_type=jnp.float32,
    )
    lane = lax.broadcasted_iota(jnp.int32, (fields, LANES), 1)
    for block in range(blocks):
        width = min(LANES, points - block * LANES)
        values = product[block * fields : (block + 1) * fields]
        inside = first_point + block * LANES + lane < count
        out_ref[:, block * LANES : block * LANES + width] = jnp.where(inside, values, 0.0)[:, :width]


def fourier_kernel(points_ref, waves_ref, arrived, out_ref, fields_ref, table_ref, left_ref):
    lats, _, points = out_ref.shape
    blocks = arrived.shape[1]
    first_point = lax.axis_index("vert") * points
    southern = lax.axis_index("wa") >= blocks // 2
    wave = waves_ref[...]
    gather_rows(arrived, fields_ref)

    def one(i, carry):
        lat = jnp.where(southern, lats - 1 - i, i)
        synthesis(
            wave, points_ref[lat], first_point, fields_ref.at[i], table_ref, left_ref, out_ref.at[lat]
        )
        return carry

    lax.fori_loop(0, lats, one, 0)


def fourier_step(arrived, waves, points, points_device):
    columns, blocks, groups, lats, _ = arrived.shape
    fields = columns * groups // 2
    rows = pl.cdiv(points_device, LANES) * fields
    return pl.pallas_call(
        fourier_kernel,
        out_shape=jax.ShapeDtypeStruct((lats, fields, points_device), jnp.float32),
        in_specs=[
            pl.BlockSpec(memory_space=pltpu.SMEM),
            pl.BlockSpec(memory_space=pltpu.VMEM),
            pl.BlockSpec(memory_space=pltpu.VMEM),
        ],
        out_specs=pl.BlockSpec(memory_space=pltpu.VMEM),
        scratch_shapes=[
            pltpu.VMEM((lats, 2, fields, M), jnp.float32),
            pltpu.VMEM((LANES, 2 * M), jnp.bfloat16),
            pltpu.VMEM((rows, 2 * M), jnp.bfloat16),
        ],
        name="fourier",
    )(points, waves, arrived)


def body(spectra, legendre, pair_waves, points):
    blocks, columns = lax.axis_size("wa"), lax.axis_size("vert")
    pair_count = legendre.shape[0]
    bounds = lax.dynamic_slice_in_dim(pair_waves, lax.axis_index("wa") * pair_count, pair_count)
    lower = pair_waves.reshape(blocks, 1, pair_count)
    waves = jnp.concatenate([lower, M - 1 - lower], axis=1).reshape(1, -1).astype(jnp.float32)
    step_length = 8 * columns
    points_device = 8 * ((4 * M + 16 + step_length - 1) // step_length)
    sent = legendre_step(spectra, jnp.swapaxes(legendre, 1, 2), bounds, blocks)
    banded = lax.all_to_all(sent, "wa", split_axis=0, concat_axis=0, tiled=True)
    spread = jnp.broadcast_to(banded[None], (columns,) + banded.shape)
    arrived = lax.all_to_all(spread, "vert", split_axis=0, concat_axis=0, tiled=True)
    return fourier_step(arrived, waves, points, points_device)


def solution(mesh):
    in_specs = (P("wa", None, "vert", None), P("wa", None, None), P(), P("wa"))
    out_specs = P("wa", None, "vert")
    return jax.shard_map(body, mesh=mesh, in_specs=in_specs, out_specs=out_specs, check_vma=False)
```

```python
import functools
import math

import jax
import jax.numpy as jnp
from jax import lax
from jax.experimental import pallas as pl
from jax.experimental.pallas import tpu as pltpu
from jax.sharding import PartitionSpec as P

M = 1280
LANES = 128
MESH = pl.DeviceIdType.MESH
SIN_PI = (
    math.pi,
    -math.pi**3 / 6,
    math.pi**5 / 120,
    -math.pi**7 / 5040,
    math.pi**9 / 362880,
    -math.pi**11 / 39916800,
    math.pi**13 / 6227020800,
)

COS_PI = (
    1.0,
    -math.pi**2 / 2,
    math.pi**4 / 24,
    -math.pi**6 / 720,
    math.pi**8 / 40320,
    -math.pi**10 / 3628800,
    math.pi**12 / 479001600,
)


def packing(waves, groups):
    full, rest = divmod(waves, LANES)
    per_slot = LANES // rest if rest else 1
    slots = full * groups + (-(-groups // per_slot) if rest else 0)
    return full, rest, per_slot, slots


def packed_order(waves):
    cut = waves.shape[1] // LANES * LANES
    return jnp.concatenate([waves[:, :cut].reshape(-1), waves[:, cut:].reshape(-1)])


def legendre_kernel(pair_block, bounds_ref, spectra_ref, legendre_ref, out_ref, scratch):
    step = pl.program_id(0)
    parts, fields, padded = spectra_ref.shape[1:]
    half = parts * fields
    heights = legendre_ref.shape[1]
    shape = (2 * half, padded)
    column = lax.broadcasted_iota(jnp.int32, shape, 1)
    plain = lax.broadcasted_iota(jnp.int32, shape, 0) < half
    alternating = jnp.where(plain | (column % 2 == 0), 1.0, -1.0)
    for i in range(pair_block):
        pair = step * pair_block + i
        boundary = M - bounds_ref[pair]
        flip = jnp.where(boundary % 2 == 0, 1.0, -1.0)
        rows = [spectra_ref[i, part].astype(jnp.float32) for part in range(parts)]
        signed = jnp.concatenate(rows + rows, axis=0) * alternating
        first = jnp.where(column < boundary, signed, 0.0)
        second = jnp.where((column >= boundary) & (column < M + 1), signed, 0.0)
        second = second * jnp.where(plain, 1.0, flip)
        masked = jnp.concatenate([first, second], axis=0).astype(jnp.bfloat16)
        scratch[pair, :, 0:heights] = lax.dot_general(
            masked,
            legendre_ref[i],
            (((1,), (1,)), ((), ())),
            preferred_element_type=jnp.float32,
        )

    @pl.when(step == pl.num_programs(0) - 1)
    def _():
        blocks, _, lats, _ = out_ref.shape
        full, rest, per_slot, _ = packing(2 * scratch.shape[0], half)
        for sign in range(2):
            rows = []
            for row in range(half):
                halves = []
                for part in range(2):
                    picked = scratch[:, (part * 2 + sign) * half + row, :]
                    halves.append(jnp.transpose(picked)[:heights])
                rows.append(jnp.concatenate(halves, axis=1))
            slots = [
                rows[row][:, chunk * LANES : (chunk + 1) * LANES]
                for chunk in range(full)
                for row in range(half)
            ]
            if rest:
                for at in range(0, half, per_slot):
                    pieces = [row[:, full * LANES :] for row in rows[at : at + per_slot]]
                    spare = LANES - rest * len(pieces)
                    if spare:
                        pieces.append(jnp.zeros((heights, spare), jnp.float32))
                    slots.append(jnp.concatenate(pieces, axis=1))
            for slot, values in enumerate(slots):
                values = values.astype(jnp.bfloat16)
                for b in range(blocks // 2):
                    target = b if sign == 0 else blocks - 1 - b
                    out_ref[target, slot] = values[b * lats : (b + 1) * lats]


def legendre_step(spectra, legendre, bounds, blocks):
    pairs, parts, fields, padded = spectra.shape
    heights = legendre.shape[1]
    block = 8 if pairs % 8 == 0 else 4
    lats = 2 * heights // blocks
    slots = packing(2 * pairs, parts * fields)[3]
    result = (blocks, slots, lats, LANES)
    return pl.pallas_call(
        functools.partial(legendre_kernel, block),
        out_shape=jax.ShapeDtypeStruct(result, jnp.bfloat16),
        grid=(pairs // block,),
        in_specs=[
            pl.BlockSpec(memory_space=pltpu.SMEM),
            pl.BlockSpec((block, parts, fields, padded), lambda i: (i, 0, 0, 0)),
            pl.BlockSpec((block, heights, padded), lambda i: (i, 0, 0)),
        ],
        out_specs=pl.BlockSpec(result, lambda i: (0, 0, 0, 0)),
        scratch_shapes=[
            pltpu.VMEM((pairs, 4 * parts * fields, max(heights, LANES)), jnp.float32)
        ],
        name="legendre",
    )(bounds, spectra, legendre)


def trig(wave, offset, length, inverse):
    product = wave * offset
    turns = (product - jnp.round(product * inverse) * length) * inverse
    square = turns * turns
    sine = jnp.float32(SIN_PI[-1])
    for term in SIN_PI[-2::-1]:
        sine = sine * square + term
    sine = sine * turns
    cosine = jnp.float32(COS_PI[-1])
    for term in COS_PI[-2::-1]:
        cosine = cosine * square + term
    return 1.0 - 2.0 * sine * sine, 2.0 * sine * cosine


def gather_rows(arrived, fields_ref, groups, waves):
    columns, blocks, _, lats, _ = arrived.shape
    full, rest, per_slot, _ = packing(waves, groups)
    half = groups // 2
    for v in range(columns):
        for g in range(groups):
            pieces = [
                arrived[v, w, chunk * groups + g].astype(jnp.float32)
                for w in range(blocks)
                for chunk in range(full)
            ]
            if rest:
                slot, at = full * groups + g // per_slot, g % per_slot * rest
                ends = [arrived[v, w, slot].astype(jnp.float32) for w in range(blocks)]
                pieces += [end[:, at : at + rest] for end in ends]
            fields_ref[:, g // half, v * half + g % half, :] = jnp.concatenate(pieces, axis=1)


def tables_of(wave, length, inverse, table_ref):
    row = lax.broadcasted_iota(jnp.int32, (8, 1), 0).astype(jnp.float32)
    fine_cos, fine_sin = trig(wave, row, length, inverse)
    for top in range(LANES // 64):
        coarse_cos, coarse_sin = trig(wave, 64 * top + 8 * row, length, inverse)
        for pair in range(4):
            cosines, sines = [], []
            for a in (2 * pair, 2 * pair + 1):
                c, s = coarse_cos[a : a + 1], coarse_sin[a : a + 1]
                cosines.append(c * fine_cos - s * fine_sin)
                sines.append(-(s * fine_cos + c * fine_sin))
            at = 64 * top + 16 * pair
            table_ref[at : at + 16, 0:M] = jnp.concatenate(cosines, axis=0).astype(jnp.bfloat16)
            table_ref[at : at + 16, M : 2 * M] = jnp.concatenate(sines, axis=0).astype(jnp.bfloat16)


def synthesis(wave, count, first_point, fields_ref, table_ref, left_ref, out_ref):
    length = count.astype(jnp.float32)
    inverse = 1.0 / length
    fields, points = out_ref.shape
    weight = jnp.where(wave == 0, 1.0, jnp.where(2 * wave < length, 2.0, 0.0))
    row = lax.broadcasted_iota(jnp.int32, (8, 1), 0).astype(jnp.float32)
    start = first_point.astype(jnp.float32)
    blocks = pl.cdiv(points, LANES)
    for block in range(blocks):
        if block % 8 == 0:
            block_cos, block_sin = trig(wave, start + LANES * (block + row), length, inverse)
            block_cos, block_sin = block_cos * weight, block_sin * weight
        c = block_cos[block % 8 : block % 8 + 1]
        s = block_sin[block % 8 : block % 8 + 1]
        real, imag = fields_ref[0], fields_ref[1]
        at = block * fields
        left_ref[at : at + fields, 0:M] = (real * c - imag * s).astype(jnp.bfloat16)
        left_ref[at : at + fields, M : 2 * M] = (real * s + imag * c).astype(jnp.bfloat16)
    product = lax.dot_general(
        left_ref[...],
        table_ref[...],
        (((1,), (1,)), ((), ())),
        preferred_element_type=jnp.float32,
    )
    lane = lax.broadcasted_iota(jnp.int32, (fields, LANES), 1)
    for block in range(blocks):
        width = min(LANES, points - block * LANES)
        values = product[block * fields : (block + 1) * fields]
        inside = first_point + block * LANES + lane < count
        out_ref[:, block * LANES : block * LANES + width] = jnp.where(inside, values, 0.0)[:, :width]


def fourier_kernel(
    groups, points_ref, waves_ref, sent, out_ref,
    arrived, fields_ref, tables_ref, left_ref,
    own_sem, send_band, recv_band, send_level, recv_level,
):
    lats, _, points = out_ref.shape
    columns, blocks = arrived.shape[:2]
    me, level = lax.axis_index("wa"), lax.axis_index("vert")
    barrier = pltpu.get_barrier_semaphore()

    def greet_band(d, carry):
        pl.semaphore_signal(
            barrier, inc=1, device_id=(lax.rem(me + d, blocks), level), device_id_type=MESH
        )
        return carry

    def greet_level(e, carry):
        pl.semaphore_signal(
            barrier, inc=1, device_id=(me, lax.rem(level + e, columns)), device_id_type=MESH
        )
        return carry

    lax.fori_loop(1, blocks, greet_band, 0)
    lax.fori_loop(1, columns, greet_level, 0)
    pl.semaphore_wait(barrier, blocks + columns - 2)

    def band_copy(d):
        target = lax.rem(me + d, blocks)
        return pltpu.make_async_remote_copy(
            src_ref=sent.at[target],
            dst_ref=arrived.at[level, me],
            send_sem=send_band.at[d],
            recv_sem=recv_band.at[d],
            device_id=(target, level),
            device_id_type=MESH,
        )

    def band_arrival(d):
        source = lax.rem(me + blocks - d, blocks)
        return pltpu.make_async_remote_copy(
            src_ref=sent.at[source],
            dst_ref=arrived.at[level, source],
            send_sem=send_band.at[d],
            recv_sem=recv_band.at[d],
            device_id=(source, level),
            device_id_type=MESH,
        )

    def level_copy(d, e):
        source = lax.rem(me + blocks - d, blocks)
        return pltpu.make_async_remote_copy(
            src_ref=arrived.at[level, source],
            dst_ref=arrived.at[level, source],
            send_sem=send_level.at[d, e],
            recv_sem=recv_level.at[d, e],
            device_id=(me, lax.rem(level + e, columns)),
            device_id_type=MESH,
        )

    def level_arrival(d, e):
        source, column = lax.rem(me + blocks - d, blocks), lax.rem(level + columns - e, columns)
        return pltpu.make_async_remote_copy(
            src_ref=arrived.at[column, source],
            dst_ref=arrived.at[column, source],
            send_sem=send_level.at[d, e],
            recv_sem=recv_level.at[d, e],
            device_id=(me, column),
            device_id_type=MESH,
        )

    def start_band(d, carry):
        band_copy(d).start()
        return carry

    own = pltpu.make_async_copy(sent.at[me], arrived.at[level, me], own_sem)
    own.start()
    lax.fori_loop(1, blocks, start_band, 0)

    wave = waves_ref[...]
    southern = me >= blocks // 2

    def lat_of(i):
        return jnp.where(southern, lats - 1 - i, i)

    def make_tables(i, carry):
        length = points_ref[lat_of(i)].astype(jnp.float32)
        tables_of(wave, length, 1.0 / length, tables_ref.at[i])
        return carry

    def start_levels(d):
        def start_level(e, carry):
            level_copy(d, e).start()
            return carry

        lax.fori_loop(1, columns, start_level, 0)

    def forward(d, carry):
        band_arrival(d).wait_recv()
        start_levels(d)
        return carry

    own.wait()
    start_levels(0)
    early = lats // 4
    lax.fori_loop(0, early, make_tables, 0)
    lax.fori_loop(1, blocks, forward, 0)
    lax.fori_loop(early, lats, make_tables, 0)

    def finish_level(d, carry):
        def finish(e, inner):
            level_arrival(d, e).wait_recv()
            level_copy(d, e).wait_send()
            return inner

        return lax.fori_loop(1, columns, finish, carry)

    def finish_band(d, carry):
        band_copy(d).wait_send()
        return carry

    lax.fori_loop(0, blocks, finish_level, 0)
    lax.fori_loop(1, blocks, finish_band, 0)
    gather_rows(arrived, fields_ref, groups, M // blocks)

    def one(i, carry):
        lat = lat_of(i)
        synthesis(
            wave,
            points_ref[lat],
            level * points,
            fields_ref.at[i],
            tables_ref.at[i],
            left_ref,
            out_ref.at[lat],
        )
        return carry

    lax.fori_loop(0, lats, one, 0)


def fourier_step(sent, waves, points, points_device, groups, columns):
    blocks, slots, lats, _ = sent.shape
    fields = columns * groups // 2
    rows = pl.cdiv(points_device, LANES) * fields
    return pl.pallas_call(
        functools.partial(fourier_kernel, groups),
        out_shape=jax.ShapeDtypeStruct((lats, fields, points_device), jnp.float32),
        in_specs=[
            pl.BlockSpec(memory_space=pltpu.SMEM),
            pl.BlockSpec(memory_space=pltpu.VMEM),
            pl.BlockSpec(memory_space=pl.ANY),
        ],
        out_specs=pl.BlockSpec(memory_space=pltpu.VMEM),
        scratch_shapes=[
            pltpu.VMEM((columns, blocks, slots, lats, LANES), jnp.bfloat16),
            pltpu.VMEM((lats, 2, fields, M), jnp.float32),
            pltpu.VMEM((lats, LANES, 2 * M), jnp.bfloat16),
            pltpu.VMEM((rows, 2 * M), jnp.bfloat16),
            pltpu.SemaphoreType.DMA,
            pltpu.SemaphoreType.DMA((blocks,)),
            pltpu.SemaphoreType.DMA((blocks,)),
            pltpu.SemaphoreType.DMA((blocks, columns)),
            pltpu.SemaphoreType.DMA((blocks, columns)),
        ],
        compiler_params=pltpu.CompilerParams(collective_id=0, has_side_effects=True),
        name="fourier",
    )(points, waves, sent)


def body(spectra, legendre, pair_waves, points):
    blocks, columns = lax.axis_size("wa"), lax.axis_size("vert")
    pair_count = legendre.shape[0]
    bounds = lax.dynamic_slice_in_dim(pair_waves, lax.axis_index("wa") * pair_count, pair_count)
    lower = pair_waves.reshape(blocks, pair_count)
    waves = packed_order(jnp.concatenate([lower, M - 1 - lower], axis=1))
    waves = waves.reshape(1, -1).astype(jnp.float32)
    step_length = 8 * columns
    points_device = 8 * ((4 * M + 16 + step_length - 1) // step_length)
    sent = legendre_step(spectra, jnp.swapaxes(legendre, 1, 2), bounds, blocks)
    groups = spectra.shape[1] * spectra.shape[2]
    return fourier_step(sent, waves, points, points_device, groups, columns)


def solution(mesh):
    in_specs = (P("wa", None, "vert", None), P("wa", None, None), P(), P("wa"))
    out_specs = P("wa", None, "vert")
    return jax.shard_map(body, mesh=mesh, in_specs=in_specs, out_specs=out_specs, check_vma=False)
```

```python
import functools
import math

import jax
import jax.numpy as jnp
from jax import lax
from jax.experimental import pallas as pl
from jax.experimental.pallas import tpu as pltpu
from jax.sharding import PartitionSpec as P

M = 1280
LANES = 128
MESH = pl.DeviceIdType.MESH
SIN_PI = (
    math.pi,
    -math.pi**3 / 6,
    math.pi**5 / 120,
    -math.pi**7 / 5040,
    math.pi**9 / 362880,
    -math.pi**11 / 39916800,
    math.pi**13 / 6227020800,
)

COS_PI = (
    1.0,
    -math.pi**2 / 2,
    math.pi**4 / 24,
    -math.pi**6 / 720,
    math.pi**8 / 40320,
    -math.pi**10 / 3628800,
    math.pi**12 / 479001600,
)


def packing(waves, groups):
    full, rest = divmod(waves, LANES)
    per_slot = LANES // rest if rest else 1
    slots = full * groups + (-(-groups // per_slot) if rest else 0)
    return full, rest, per_slot, slots


def packed_order(pairs, blocks):
    count = pairs.shape[1] // blocks
    cut = 2 * count // LANES * LANES
    waves = []
    for block in range(blocks):
        lower = pairs[:, block * count : (block + 1) * count]
        waves.append(jnp.concatenate([lower, M - 1 - lower], axis=1))
    heads = [wave[:, :cut] for wave in waves] if cut else []
    tails = [wave[:, cut:] for wave in waves] if cut < 2 * count else []
    return jnp.concatenate(heads + tails, axis=1)


def legendre_kernel(pair_block, waves_ref, spectra_ref, legendre_ref, out_ref, scratch):
    step = pl.program_id(0)
    parts, fields, padded = spectra_ref.shape[1:]
    half = parts * fields
    heights = legendre_ref.shape[1]
    num_pairs = scratch.shape[0]
    shape = (2 * half, padded)
    column = lax.broadcasted_iota(jnp.int32, shape, 1)
    plain = lax.broadcasted_iota(jnp.int32, shape, 0) < half
    alternating = jnp.where(plain | (column % 2 == 0), 1.0, -1.0)
    for i in range(pair_block):
        pair = step * pair_block + i
        boundary = M - waves_ref[lax.axis_index("wa") * num_pairs + pair]
        flip = jnp.where(boundary % 2 == 0, 1.0, -1.0)
        rows = [spectra_ref[i, part].astype(jnp.float32) for part in range(parts)]
        signed = jnp.concatenate(rows + rows, axis=0) * alternating
        first = jnp.where(column < boundary, signed, 0.0)
        second = jnp.where((column >= boundary) & (column < M + 1), signed, 0.0)
        second = second * jnp.where(plain, 1.0, flip)
        masked = jnp.concatenate([first, second], axis=0).astype(jnp.bfloat16)
        scratch[pair, :, 0:heights] = lax.dot_general(
            masked,
            legendre_ref[i],
            (((1,), (1,)), ((), ())),
            preferred_element_type=jnp.float32,
        )

    @pl.when(step == pl.num_programs(0) - 1)
    def _():
        blocks, _, lats, _ = out_ref.shape
        full, rest, per_slot, _ = packing(2 * scratch.shape[0], half)
        for sign in range(2):
            rows = []
            for row in range(half):
                halves = []
                for part in range(2):
                    picked = scratch[:, (part * 2 + sign) * half + row, :]
                    halves.append(jnp.transpose(picked)[:heights])
                rows.append(jnp.concatenate(halves, axis=1))
            slots = [
                rows[row][:, chunk * LANES : (chunk + 1) * LANES]
                for chunk in range(full)
                for row in range(half)
            ]
            if rest:
                for at in range(0, half, per_slot):
                    pieces = [row[:, full * LANES :] for row in rows[at : at + per_slot]]
                    spare = LANES - rest * len(pieces)
                    if spare:
                        pieces.append(jnp.zeros((heights, spare), jnp.float32))
                    slots.append(jnp.concatenate(pieces, axis=1))
            for slot, values in enumerate(slots):
                values = values.astype(jnp.bfloat16)
                for b in range(blocks // 2):
                    target = b if sign == 0 else blocks - 1 - b
                    out_ref[target, slot] = values[b * lats : (b + 1) * lats]


def legendre_step(spectra, legendre, pair_waves, blocks):
    pairs, parts, fields, padded = spectra.shape
    heights = legendre.shape[1]
    block = 8 if pairs % 8 == 0 else 4
    lats = 2 * heights // blocks
    slots = packing(2 * pairs, parts * fields)[3]
    result = (blocks, slots, lats, LANES)
    return pl.pallas_call(
        functools.partial(legendre_kernel, block),
        out_shape=jax.ShapeDtypeStruct(result, jnp.bfloat16),
        grid=(pairs // block,),
        in_specs=[
            pl.BlockSpec(memory_space=pltpu.SMEM),
            pl.BlockSpec((block, parts, fields, padded), lambda i: (i, 0, 0, 0)),
            pl.BlockSpec((block, heights, padded), lambda i: (i, 0, 0)),
        ],
        out_specs=pl.BlockSpec(result, lambda i: (0, 0, 0, 0)),
        scratch_shapes=[
            pltpu.VMEM((pairs, 4 * parts * fields, max(heights, LANES)), jnp.float32)
        ],
        name="legendre",
    )(pair_waves, spectra, legendre)


def trig(wave, offset, length, inverse):
    product = wave * offset
    turns = (product - jnp.round(product * inverse) * length) * inverse
    square = turns * turns
    sine = jnp.float32(SIN_PI[-1])
    for term in SIN_PI[-2::-1]:
        sine = sine * square + term
    sine = sine * turns
    cosine = jnp.float32(COS_PI[-1])
    for term in COS_PI[-2::-1]:
        cosine = cosine * square + term
    return 1.0 - 2.0 * sine * sine, 2.0 * sine * cosine


def gather_rows(arrived, fields_ref, groups, waves):
    blocks = arrived.shape[0]
    full, rest, per_slot, _ = packing(waves, groups)
    for g in range(groups):
        pieces = [
            arrived[w, chunk * groups + g].astype(jnp.float32)
            for w in range(blocks)
            for chunk in range(full)
        ]
        if rest:
            slot, at = full * groups + g // per_slot, g % per_slot * rest
            ends = [arrived[w, slot].astype(jnp.float32) for w in range(blocks)]
            pieces += [end[:, at : at + rest] for end in ends]
        fields_ref[:, g, :] = jnp.concatenate(pieces, axis=1)


def tables_of(wave, length, inverse, table_ref):
    row = lax.broadcasted_iota(jnp.int32, (8, 1), 0).astype(jnp.float32)
    fine_cos, fine_sin = trig(wave, row, length, inverse)
    for top in range(LANES // 64):
        coarse_cos, coarse_sin = trig(wave, 64 * top + 8 * row, length, inverse)
        for pair in range(4):
            cosines, sines = [], []
            for a in (2 * pair, 2 * pair + 1):
                c, s = coarse_cos[a : a + 1], coarse_sin[a : a + 1]
                cosines.append(c * fine_cos - s * fine_sin)
                sines.append(-(s * fine_cos + c * fine_sin))
            at = 64 * top + 16 * pair
            table_ref[at : at + 16, 0:M] = jnp.concatenate(cosines, axis=0).astype(jnp.bfloat16)
            table_ref[at : at + 16, M : 2 * M] = jnp.concatenate(sines, axis=0).astype(jnp.bfloat16)


def synthesis(wave, count, columns, points, fields, table_ref, left_ref):
    length = count.astype(jnp.float32)
    inverse = 1.0 / length
    local = fields.shape[0] // 2
    rows = columns * local
    weight = jnp.where(wave == 0, 1.0, jnp.where(2 * wave < length, 2.0, 0.0))
    column = (lax.broadcasted_iota(jnp.int32, (rows, 1), 0) // local).astype(jnp.float32)
    cosine, sine = trig(wave, points * column, length, inverse)
    real = jnp.concatenate([fields[:local] * weight] * columns, axis=0)
    imag = jnp.concatenate([fields[local:] * weight] * columns, axis=0)
    real, imag = real * cosine - imag * sine, real * sine + imag * cosine
    row = lax.broadcasted_iota(jnp.int32, (8, 1), 0).astype(jnp.float32)
    for block in range(pl.cdiv(points, LANES)):
        if block % 8 == 0:
            block_cos, block_sin = trig(wave, LANES * (block + row), length, inverse)
        c = block_cos[block % 8 : block % 8 + 1]
        s = block_sin[block % 8 : block % 8 + 1]
        at = block * rows
        left_ref[at : at + rows, 0:M] = (real * c - imag * s).astype(jnp.bfloat16)
        left_ref[at : at + rows, M : 2 * M] = (real * s + imag * c).astype(jnp.bfloat16)
    return lax.dot_general(
        left_ref[...],
        table_ref[...],
        (((1,), (1,)), ((), ())),
        preferred_element_type=jnp.float32,
    )


def slot_latitude(i, lats, blocks):
    return jnp.where(lax.axis_index("wa") >= blocks // 2, lats - 1 - i, i)


def fourier_kernel(
    groups, points, points_ref, pairs_ref, sent, landed,
    arrived, fields_ref, tables_ref, left_ref, sums_ref, leaving,
    own_sem, send_band, recv_band, send_level, recv_level,
):
    lats = tables_ref.shape[0]
    columns, parts = landed.shape[:2]
    blocks = arrived.shape[0]
    local = groups // 2
    me, level = lax.axis_index("wa"), lax.axis_index("vert")
    barrier = pltpu.get_barrier_semaphore()

    def greet_band(d, carry):
        pl.semaphore_signal(
            barrier, inc=1, device_id=(lax.rem(me + d, blocks), level), device_id_type=MESH
        )
        return carry

    def greet_level(e, carry):
        pl.semaphore_signal(
            barrier, inc=1, device_id=(me, lax.rem(level + e, columns)), device_id_type=MESH
        )
        return carry

    lax.fori_loop(1, blocks, greet_band, 0)
    lax.fori_loop(1, columns, greet_level, 0)
    own = pltpu.make_async_copy(sent.at[me], arrived.at[me], own_sem.at[0])
    own.start()
    pl.semaphore_wait(barrier, blocks + columns - 2)

    def band_copy(d):
        target = lax.rem(me + d, blocks)
        return pltpu.make_async_remote_copy(
            src_ref=sent.at[target],
            dst_ref=arrived.at[me],
            send_sem=send_band.at[d],
            recv_sem=recv_band.at[d],
            device_id=(target, level),
            device_id_type=MESH,
        )

    def band_arrival(d):
        source = lax.rem(me + blocks - d, blocks)
        return pltpu.make_async_remote_copy(
            src_ref=sent.at[source],
            dst_ref=arrived.at[source],
            send_sem=send_band.at[d],
            recv_sem=recv_band.at[d],
            device_id=(source, level),
            device_id_type=MESH,
        )

    def level_copy(part, e):
        target = lax.rem(level + e, columns)
        return pltpu.make_async_remote_copy(
            src_ref=leaving.at[part, target],
            dst_ref=landed.at[level, part],
            send_sem=send_level.at[part, e],
            recv_sem=recv_level.at[part, e],
            device_id=(me, target),
            device_id_type=MESH,
        )

    def level_arrival(part, e):
        source = lax.rem(level + columns - e, columns)
        return pltpu.make_async_remote_copy(
            src_ref=leaving.at[part, source],
            dst_ref=landed.at[source, part],
            send_sem=send_level.at[part, e],
            recv_sem=recv_level.at[part, e],
            device_id=(me, source),
            device_id_type=MESH,
        )

    def start_band(d, carry):
        band_copy(d).start()
        return carry

    lax.fori_loop(1, blocks, start_band, 0)
    wave = packed_order(pairs_ref[...].astype(jnp.float32), blocks)

    def make_tables(i, carry):
        length = points_ref[slot_latitude(i, lats, blocks)].astype(jnp.float32)
        tables_of(wave, length, 1.0 / length, tables_ref.at[i])
        return carry

    lax.fori_loop(0, lats, make_tables, 0)
    own.wait()

    def finish_band(d, carry):
        band_arrival(d).wait_recv()
        band_copy(d).wait_send()
        return carry

    lax.fori_loop(1, blocks, finish_band, 0)
    gather_rows(arrived, fields_ref, groups, M // blocks)
    each = lats // parts
    rows = columns * local

    def one_part(part, carry):
        for j in range(each):
            i = part * each + j
            product = synthesis(
                wave,
                points_ref[slot_latitude(i, lats, blocks)],
                columns,
                points,
                fields_ref[i],
                tables_ref.at[i],
                left_ref,
            )
            for block in range(product.shape[0] // rows):
                for v in range(columns):
                    at = block * rows + v * local
                    sums_ref[v, j * local : (j + 1) * local, block * LANES : (block + 1) * LANES] = (
                        product[at : at + local]
                    )
        for v in range(columns):
            leaving[part, v] = sums_ref[v].astype(jnp.bfloat16)

        def start_level(e, inner):
            level_copy(part, e).start()
            return inner

        lax.fori_loop(1, columns, start_level, 0)
        pltpu.make_async_copy(
            leaving.at[part, level], landed.at[level, part], own_sem.at[1 + part]
        ).start()
        return carry

    lax.fori_loop(0, parts, one_part, 0)

    def finish_part(part, carry):
        def finish(e, inner):
            level_arrival(part, e).wait_recv()
            level_copy(part, e).wait_send()
            return inner

        pltpu.make_async_copy(
            leaving.at[part, level], landed.at[level, part], own_sem.at[1 + part]
        ).wait()
        return lax.fori_loop(1, columns, finish, carry)

    lax.fori_loop(0, parts, finish_part, 0)


def fourier_step(sent, pair_waves, points, points_device, groups, columns):
    blocks, slots, lats, _ = sent.shape
    local = groups // 2
    parts = 2
    chunks = pl.cdiv(points_device, LANES)
    rows = lats // parts * local
    return pl.pallas_call(
        functools.partial(fourier_kernel, groups, points_device),
        out_shape=jax.ShapeDtypeStruct((columns, parts, rows, chunks * LANES), jnp.bfloat16),
        in_specs=[
            pl.BlockSpec(memory_space=pltpu.SMEM),
            pl.BlockSpec(memory_space=pltpu.VMEM),
            pl.BlockSpec(memory_space=pl.ANY),
        ],
        out_specs=pl.BlockSpec(memory_space=pl.ANY),
        scratch_shapes=[
            pltpu.VMEM((blocks, slots, lats, LANES), jnp.bfloat16),
            pltpu.VMEM((lats, groups, M), jnp.float32),
            pltpu.VMEM((lats, LANES, 2 * M), jnp.bfloat16),
            pltpu.VMEM((chunks * columns * local, 2 * M), jnp.bfloat16),
            pltpu.VMEM((columns, rows, chunks * LANES), jnp.float32),
            pltpu.VMEM((parts, columns, rows, chunks * LANES), jnp.bfloat16),
            pltpu.SemaphoreType.DMA((1 + parts,)),
            pltpu.SemaphoreType.DMA((blocks,)),
            pltpu.SemaphoreType.DMA((blocks,)),
            pltpu.SemaphoreType.DMA((parts, columns)),
            pltpu.SemaphoreType.DMA((parts, columns)),
        ],
        compiler_params=pltpu.CompilerParams(collective_id=0, has_side_effects=True),
        name="fourier",
    )(points, pair_waves.reshape(1, -1), sent)


def place_kernel(blocks, points_ref, landed, out_ref):
    lats, fields, points = out_ref.shape
    columns, parts = landed.shape[:2]
    each, local = lats // parts, fields // columns
    first_point = lax.axis_index("vert") * points
    for part in range(parts):
        values = [landed[v, part].astype(jnp.float32) for v in range(columns)]
        for j in range(each):
            lat = slot_latitude(part * each + j, lats, blocks)
            rows = jnp.concatenate([value[j * local : (j + 1) * local] for value in values], axis=0)
            index = first_point + lax.broadcasted_iota(jnp.int32, rows.shape, 1)
            out_ref[lat] = jnp.where(index < points_ref[lat], rows, 0.0)[:, :points]


def place_step(landed, points, points_device, lats, fields, blocks):
    return pl.pallas_call(
        functools.partial(place_kernel, blocks),
        out_shape=jax.ShapeDtypeStruct((lats, fields, points_device), jnp.float32),
        in_specs=[
            pl.BlockSpec(memory_space=pltpu.SMEM),
            pl.BlockSpec(memory_space=pltpu.VMEM),
        ],
        out_specs=pl.BlockSpec(memory_space=pltpu.VMEM),
        name="place",
    )(points, landed)


def body(spectra, legendre, pair_waves, points):
    blocks, columns = lax.axis_size("wa"), lax.axis_size("vert")
    step_length = 8 * columns
    points_device = 8 * ((4 * M + 16 + step_length - 1) // step_length)
    groups = spectra.shape[1] * spectra.shape[2]
    sent = legendre_step(spectra, jnp.swapaxes(legendre, 1, 2), pair_waves, blocks)
    landed = fourier_step(sent, pair_waves, points, points_device, groups, columns)
    fields = columns * groups // 2
    return place_step(landed, points, points_device, points.shape[0], fields, blocks)


def solution(mesh):
    in_specs = (P("wa", None, "vert", None), P("wa", None, None), P(), P("wa"))
    out_specs = P("wa", None, "vert")
    return jax.shard_map(body, mesh=mesh, in_specs=in_specs, out_specs=out_specs, check_vma=False)
```

```python
import functools

import jax
import jax.numpy as jnp
from jax import lax
from jax.experimental import pallas as pl
from jax.experimental.pallas import tpu as pltpu
from jax.sharding import PartitionSpec as P

M = 1280
LANES = 128
MESH = pl.DeviceIdType.MESH
SIN_PI = (3.141592640183955, -5.167710090327305, 2.5500776596396157, -0.5982921588969844, 0.07765940708214343)
COS_PI = (0.9999999534665123, -4.934792858655412, 4.058411913769657, -1.3318801587031317, 0.21969679350917085)


def packing(waves, groups):
    full, rest = divmod(waves, LANES)
    per_slot = LANES // rest if rest else 1
    slots = full * groups + (-(-groups // per_slot) if rest else 0)
    return full, rest, per_slot, slots


def packed_order(pairs, blocks):
    count = pairs.shape[1] // blocks
    cut = 2 * count // LANES * LANES
    waves = []
    for block in range(blocks):
        lower = pairs[:, block * count : (block + 1) * count]
        waves.append(jnp.concatenate([lower, M - 1 - lower], axis=1))
    heads = [wave[:, :cut] for wave in waves] if cut else []
    tails = [wave[:, cut:] for wave in waves] if cut < 2 * count else []
    return jnp.concatenate(heads + tails, axis=1)


def legendre_kernel(pair_block, waves_ref, spectra_ref, legendre_ref, out_ref, scratch, patterns):
    step = pl.program_id(0)
    parts, fields, padded = spectra_ref.shape[1:]
    half = parts * fields
    heights = legendre_ref.shape[1]
    num_pairs = scratch.shape[0]
    column = lax.broadcasted_iota(jnp.int32, (8, padded), 1)
    row = lax.broadcasted_iota(jnp.int32, (8, padded), 0)

    @pl.when(step == 0)
    def _():
        later = (row // 2) % 2 == 1
        signed = row % 2 == 1
        plain = jnp.where(signed & (column % 2 == 1), -1.0, 1.0)
        even = jnp.where(later & (column < M + 1), plain, 0.0)
        patterns[0] = jnp.where(later, 0.0, plain)
        patterns[1] = even
        patterns[2] = jnp.where(signed, -even, even)

    for i in range(pair_block):
        pair = step * pair_block + i
        boundary = M - waves_ref[lax.axis_index("wa") * num_pairs + pair]
        pattern = jnp.where(column < boundary, patterns[0], patterns[1 + boundary % 2])
        masked = []
        for part in range(parts):
            rows = spectra_ref[i, part].astype(jnp.float32)
            for at in range(0, fields, 2):
                masked.append(jnp.where(row < 4, rows[at : at + 1], rows[at + 1 : at + 2]) * pattern)
        masked = jnp.concatenate(masked, axis=0).astype(jnp.bfloat16)
        scratch[pair, :, 0:heights] = lax.dot_general(
            masked,
            legendre_ref[i],
            (((1,), (1,)), ((), ())),
            preferred_element_type=jnp.float32,
        )

    @pl.when(step == pl.num_programs(0) - 1)
    def _():
        blocks, _, lats, _ = out_ref.shape
        full, rest, per_slot, _ = packing(2 * scratch.shape[0], half)
        for sign in range(2):
            rows = []
            for coefficient in range(half):
                halves = []
                for part in range(2):
                    picked = scratch[:, 4 * coefficient + 2 * part + sign, :]
                    halves.append(jnp.transpose(picked)[:heights])
                rows.append(jnp.concatenate(halves, axis=1))
            slots = [
                rows[row][:, chunk * LANES : (chunk + 1) * LANES]
                for chunk in range(full)
                for row in range(half)
            ]
            if rest:
                for at in range(0, half, per_slot):
                    pieces = [row[:, full * LANES :] for row in rows[at : at + per_slot]]
                    spare = LANES - rest * len(pieces)
                    if spare:
                        pieces.append(jnp.zeros((heights, spare), jnp.float32))
                    slots.append(jnp.concatenate(pieces, axis=1))
            for slot, values in enumerate(slots):
                values = values.astype(jnp.bfloat16)
                for b in range(blocks // 2):
                    target = b if sign == 0 else blocks - 1 - b
                    out_ref[target, slot] = values[b * lats : (b + 1) * lats]


def legendre_step(spectra, legendre, pair_waves, blocks):
    pairs, parts, fields, padded = spectra.shape
    heights = legendre.shape[1]
    block = 8 if pairs % 8 == 0 else 4
    lats = 2 * heights // blocks
    slots = packing(2 * pairs, parts * fields)[3]
    result = (blocks, slots, lats, LANES)
    return pl.pallas_call(
        functools.partial(legendre_kernel, block),
        out_shape=jax.ShapeDtypeStruct(result, jnp.bfloat16),
        grid=(pairs // block,),
        in_specs=[
            pl.BlockSpec(memory_space=pltpu.SMEM),
            pl.BlockSpec((block, parts, fields, padded), lambda i: (i, 0, 0, 0)),
            pl.BlockSpec((block, heights, padded), lambda i: (i, 0, 0)),
        ],
        out_specs=pl.BlockSpec(result, lambda i: (0, 0, 0, 0)),
        scratch_shapes=[
            pltpu.VMEM((pairs, 4 * parts * fields, max(heights, LANES)), jnp.float32),
            pltpu.VMEM((3, 8, padded), jnp.float32),
        ],
        name="legendre",
    )(pair_waves, spectra, legendre)


def trig(wave, offset, length, inverse):
    product = wave * offset
    turns = (product - jnp.round(product * inverse) * length) * inverse
    square = turns * turns
    sine = jnp.float32(SIN_PI[-1])
    for term in SIN_PI[-2::-1]:
        sine = sine * square + term
    sine = sine * turns
    cosine = jnp.float32(COS_PI[-1])
    for term in COS_PI[-2::-1]:
        cosine = cosine * square + term
    double = sine + sine
    return 1.0 - double * sine, double * cosine


def gather_rows(arrived, fields_ref, groups, waves):
    blocks = arrived.shape[0]
    full, rest, per_slot, _ = packing(waves, groups)
    for g in range(groups):
        pieces = [
            arrived[w, chunk * groups + g].astype(jnp.float32)
            for w in range(blocks)
            for chunk in range(full)
        ]
        if rest:
            slot, at = full * groups + g // per_slot, g % per_slot * rest
            ends = [arrived[w, slot].astype(jnp.float32) for w in range(blocks)]
            pieces += [end[:, at : at + rest] for end in ends]
        fields_ref[:, g, :] = jnp.concatenate(pieces, axis=1)


def doubled_shift(cosine, sine):
    c, s = cosine[4:5], sine[4:5]
    c, s = 1.0 - 2.0 * s * s, 2.0 * s * c
    return cosine * c - sine * s, sine * c + cosine * s


def tables_of(wave, length, inverse, table_ref):
    row = lax.broadcasted_iota(jnp.int32, (8, 1), 0).astype(jnp.float32)
    fine_cos, fine_sin = trig(wave, row, length, inverse)
    for top in range(LANES // 64):
        if top == 0:
            coarse_cos, coarse_sin = trig(wave, 8 * row, length, inverse)
        else:
            coarse_cos, coarse_sin = doubled_shift(coarse_cos, coarse_sin)
        for pair in range(4):
            cosines, sines = [], []
            for a in (2 * pair, 2 * pair + 1):
                c, s = coarse_cos[a : a + 1], coarse_sin[a : a + 1]
                cosines.append(c * fine_cos - s * fine_sin)
                sines.append(-(s * fine_cos + c * fine_sin))
            at = 64 * top + 16 * pair
            table_ref[at : at + 16, 0:M] = jnp.concatenate(cosines, axis=0).astype(jnp.bfloat16)
            table_ref[at : at + 16, M : 2 * M] = jnp.concatenate(sines, axis=0).astype(jnp.bfloat16)


def synthesis(wave, count, columns, points, fields, table_ref, left_ref):
    length = count.astype(jnp.float32)
    inverse = 1.0 / length
    local = fields.shape[0] // 2
    rows = columns * local
    weight = jnp.where(wave == 0, 1.0, jnp.where(2 * wave < length, 2.0, 0.0))
    column = (lax.broadcasted_iota(jnp.int32, (rows, 1), 0) // local).astype(jnp.float32)
    cosine, sine = trig(wave, points * column, length, inverse)
    real = jnp.concatenate([fields[:local] * weight] * columns, axis=0)
    imag = jnp.concatenate([fields[local:] * weight] * columns, axis=0)
    real, imag = real * cosine - imag * sine, real * sine + imag * cosine
    row = lax.broadcasted_iota(jnp.int32, (8, 1), 0).astype(jnp.float32)
    for block in range(pl.cdiv(points, LANES)):
        if block == 0:
            block_cos, block_sin = trig(wave, LANES * row, length, inverse)
        elif block == 8:
            block_cos, block_sin = doubled_shift(block_cos, block_sin)
        elif block % 8 == 0:
            block_cos, block_sin = trig(wave, LANES * (block + row), length, inverse)
        c = block_cos[block % 8 : block % 8 + 1]
        s = block_sin[block % 8 : block % 8 + 1]
        at = block * rows
        left_ref[at : at + rows, 0:M] = (real * c - imag * s).astype(jnp.bfloat16)
        left_ref[at : at + rows, M : 2 * M] = (real * s + imag * c).astype(jnp.bfloat16)
    return lax.dot_general(
        left_ref[...],
        table_ref[...],
        (((1,), (1,)), ((), ())),
        preferred_element_type=jnp.float32,
    )


def slot_latitude(i, lats, blocks):
    return jnp.where(lax.axis_index("wa") >= blocks // 2, lats - 1 - i, i)


def fourier_kernel(
    groups, points, points_ref, pairs_ref, sent, landed,
    arrived, fields_ref, tables_ref, left_ref, sums_ref, leaving,
    own_sem, send_band, recv_band, send_level, recv_level,
):
    lats = tables_ref.shape[0]
    columns, parts = landed.shape[:2]
    blocks = arrived.shape[0]
    local = groups // 2
    me, level = lax.axis_index("wa"), lax.axis_index("vert")
    barrier = pltpu.get_barrier_semaphore()

    def greet_band(d, carry):
        pl.semaphore_signal(
            barrier, inc=1, device_id=(lax.rem(me + d, blocks), level), device_id_type=MESH
        )
        return carry

    def greet_level(e, carry):
        pl.semaphore_signal(
            barrier, inc=1, device_id=(me, lax.rem(level + e, columns)), device_id_type=MESH
        )
        return carry

    lax.fori_loop(1, blocks, greet_band, 0)
    lax.fori_loop(1, columns, greet_level, 0)
    own = pltpu.make_async_copy(sent.at[me], arrived.at[me], own_sem.at[0])
    own.start()

    def band_copy(d):
        target = lax.rem(me + d, blocks)
        return pltpu.make_async_remote_copy(
            src_ref=sent.at[target],
            dst_ref=arrived.at[me],
            send_sem=send_band.at[d],
            recv_sem=recv_band.at[d],
            device_id=(target, level),
            device_id_type=MESH,
        )

    def band_arrival(d):
        source = lax.rem(me + blocks - d, blocks)
        return pltpu.make_async_remote_copy(
            src_ref=sent.at[source],
            dst_ref=arrived.at[source],
            send_sem=send_band.at[d],
            recv_sem=recv_band.at[d],
            device_id=(source, level),
            device_id_type=MESH,
        )

    def level_copy(part, e):
        target = lax.rem(level + e, columns)
        return pltpu.make_async_remote_copy(
            src_ref=leaving.at[part, target],
            dst_ref=landed.at[level, part],
            send_sem=send_level.at[part, e],
            recv_sem=recv_level.at[part, e],
            device_id=(me, target),
            device_id_type=MESH,
        )

    def level_arrival(part, e):
        source = lax.rem(level + columns - e, columns)
        return pltpu.make_async_remote_copy(
            src_ref=leaving.at[part, source],
            dst_ref=landed.at[source, part],
            send_sem=send_level.at[part, e],
            recv_sem=recv_level.at[part, e],
            device_id=(me, source),
            device_id_type=MESH,
        )

    def start_band(d, carry):
        band_copy(d).start()
        return carry

    wave = packed_order(pairs_ref[...].astype(jnp.float32).reshape(1, -1), blocks)

    def make_tables(i, carry):
        length = points_ref[slot_latitude(i, lats, blocks)].astype(jnp.float32)
        tables_of(wave, length, 1.0 / length, tables_ref.at[i])
        return carry

    early = lats // 4
    lax.fori_loop(0, early, make_tables, 0)
    pl.semaphore_wait(barrier, blocks + columns - 2)
    lax.fori_loop(1, blocks, start_band, 0)
    lax.fori_loop(early, lats, make_tables, 0)
    own.wait()

    def finish_band(d, carry):
        band_arrival(d).wait_recv()
        band_copy(d).wait_send()
        return carry

    lax.fori_loop(1, blocks, finish_band, 0)
    gather_rows(arrived, fields_ref, groups, M // blocks)
    each = lats // parts
    rows = columns * local

    def one_part(part, carry):
        for j in range(each):
            i = part * each + j
            product = synthesis(
                wave,
                points_ref[slot_latitude(i, lats, blocks)],
                columns,
                points,
                fields_ref[i],
                tables_ref.at[i],
                left_ref,
            )
            for block in range(product.shape[0] // rows):
                for v in range(columns):
                    at = block * rows + v * local
                    sums_ref[v, j * local : (j + 1) * local, block * LANES : (block + 1) * LANES] = (
                        product[at : at + local]
                    )
        for v in range(columns):
            leaving[part, v] = sums_ref[v].astype(jnp.bfloat16)

        def start_level(e, inner):
            level_copy(part, e).start()
            return inner

        lax.fori_loop(1, columns, start_level, 0)
        pltpu.make_async_copy(
            leaving.at[part, level], landed.at[level, part], own_sem.at[1 + part]
        ).start()
        return carry

    lax.fori_loop(0, parts, one_part, 0)

    def finish_part(part, carry):
        def finish(e, inner):
            level_arrival(part, e).wait_recv()
            level_copy(part, e).wait_send()
            return inner

        pltpu.make_async_copy(
            leaving.at[part, level], landed.at[level, part], own_sem.at[1 + part]
        ).wait()
        return lax.fori_loop(1, columns, finish, carry)

    lax.fori_loop(0, parts, finish_part, 0)


def fourier_step(sent, pair_waves, points, points_device, groups, columns):
    blocks, slots, lats, _ = sent.shape
    local = groups // 2
    parts = 2
    chunks = pl.cdiv(points_device, LANES)
    rows = lats // parts * local
    return pl.pallas_call(
        functools.partial(fourier_kernel, groups, points_device),
        out_shape=jax.ShapeDtypeStruct((columns, parts, rows, chunks * LANES), jnp.bfloat16),
        in_specs=[
            pl.BlockSpec(memory_space=pltpu.SMEM),
            pl.BlockSpec(memory_space=pltpu.VMEM),
            pl.BlockSpec(memory_space=pl.ANY),
        ],
        out_specs=pl.BlockSpec(memory_space=pl.ANY),
        scratch_shapes=[
            pltpu.VMEM((blocks, slots, lats, LANES), jnp.bfloat16),
            pltpu.VMEM((lats, groups, M), jnp.float32),
            pltpu.VMEM((lats, LANES, 2 * M), jnp.bfloat16),
            pltpu.VMEM((chunks * columns * local, 2 * M), jnp.bfloat16),
            pltpu.VMEM((columns, rows, chunks * LANES), jnp.float32),
            pltpu.VMEM((parts, columns, rows, chunks * LANES), jnp.bfloat16),
            pltpu.SemaphoreType.DMA((1 + parts,)),
            pltpu.SemaphoreType.DMA((blocks,)),
            pltpu.SemaphoreType.DMA((blocks,)),
            pltpu.SemaphoreType.DMA((parts, columns)),
            pltpu.SemaphoreType.DMA((parts, columns)),
        ],
        compiler_params=pltpu.CompilerParams(collective_id=0, has_side_effects=True),
        name="fourier",
    )(points, pair_waves, sent)


def place_kernel(blocks, points_ref, landed, out_ref):
    lats, fields, points = out_ref.shape
    columns, parts = landed.shape[:2]
    each, local = lats // parts, fields // columns
    first_point = lax.axis_index("vert") * points
    for part in range(parts):
        values = [landed[v, part].astype(jnp.float32) for v in range(columns)]
        for j in range(each):
            lat = slot_latitude(part * each + j, lats, blocks)
            rows = jnp.concatenate([value[j * local : (j + 1) * local] for value in values], axis=0)
            index = first_point + lax.broadcasted_iota(jnp.int32, rows.shape, 1)
            out_ref[lat] = jnp.where(index < points_ref[lat], rows, 0.0)[:, :points]


def place_step(landed, points, points_device, lats, fields, blocks):
    return pl.pallas_call(
        functools.partial(place_kernel, blocks),
        out_shape=jax.ShapeDtypeStruct((lats, fields, points_device), jnp.float32),
        in_specs=[
            pl.BlockSpec(memory_space=pltpu.SMEM),
            pl.BlockSpec(memory_space=pltpu.VMEM),
        ],
        out_specs=pl.BlockSpec(memory_space=pltpu.VMEM),
        name="place",
    )(points, landed)


def body(spectra, legendre, pair_waves, points):
    blocks, columns = lax.axis_size("wa"), lax.axis_size("vert")
    step_length = 8 * columns
    points_device = 8 * ((4 * M + 16 + step_length - 1) // step_length)
    groups = spectra.shape[1] * spectra.shape[2]
    sent = legendre_step(spectra, jnp.swapaxes(legendre, 1, 2), pair_waves, blocks)
    landed = fourier_step(sent, pair_waves, points, points_device, groups, columns)
    fields = columns * groups // 2
    return place_step(landed, points, points_device, points.shape[0], fields, blocks)


def solution(mesh):
    in_specs = (P("wa", None, "vert", None), P("wa", None, None), P(), P("wa"))
    out_specs = P("wa", None, "vert")
    return jax.shard_map(body, mesh=mesh, in_specs=in_specs, out_specs=out_specs, check_vma=False)
```

```python
import functools

import jax
import jax.numpy as jnp
from jax import lax
from jax.experimental import pallas as pl
from jax.experimental.pallas import tpu as pltpu
from jax.sharding import PartitionSpec as P

M = 1280
LANES = 128
MESH = pl.DeviceIdType.MESH
SIN_PI = (3.141592640183955, -5.167710090327305, 2.5500776596396157, -0.5982921588969844, 0.07765940708214343)
COS_PI = (0.9999999534665123, -4.934792858655412, 4.058411913769657, -1.3318801587031317, 0.21969679350917085)


def packing(waves, groups):
    full, rest = divmod(waves, LANES)
    per_slot = LANES // rest if rest else 1
    slots = full * groups + (-(-groups // per_slot) if rest else 0)
    return full, rest, per_slot, slots


def packed_order(pairs, blocks):
    count = pairs.shape[1] // blocks
    cut = 2 * count // LANES * LANES
    waves = []
    for block in range(blocks):
        lower = pairs[:, block * count : (block + 1) * count]
        waves.append(jnp.concatenate([lower, M - 1 - lower], axis=1))
    heads = [wave[:, :cut] for wave in waves] if cut else []
    tails = [wave[:, cut:] for wave in waves] if cut < 2 * count else []
    return jnp.concatenate(heads + tails, axis=1)


def legendre_kernel(
    pair_block, waves_ref, spectra, legendre, out_ref,
    scratch, patterns, spectra_ref, legendre_ref, sems,
):
    parts, fields, padded = spectra_ref.shape[1:]
    half = parts * fields
    heights = legendre_ref.shape[1]
    num_pairs = scratch.shape[0]
    column = lax.broadcasted_iota(jnp.int32, (8, padded), 1)
    row = lax.broadcasted_iota(jnp.int32, (8, padded), 0)

    def copies(step):
        at = pl.ds(step * pair_block, pair_block)
        return (
            pltpu.make_async_copy(spectra.at[at], spectra_ref.at[at], sems.at[0, step]),
            pltpu.make_async_copy(legendre.at[at], legendre_ref.at[at], sems.at[1, step]),
        )

    def start(step, carry):
        for copy in copies(step):
            copy.start()
        return carry

    steps = num_pairs // pair_block
    lax.fori_loop(0, steps, start, 0)

    later = (row // 2) % 2 == 1
    signed = row % 2 == 1
    plain = jnp.where(signed & (column % 2 == 1), -1.0, 1.0)
    even = jnp.where(later & (column < M + 1), plain, 0.0)
    patterns[0] = jnp.where(later, 0.0, plain)
    patterns[1] = even
    patterns[2] = jnp.where(signed, -even, even)

    def project(step, carry):
        for copy in copies(step):
            copy.wait()
        for i in range(pair_block):
            pair = step * pair_block + i
            boundary = M - waves_ref[lax.axis_index("wa") * num_pairs + pair]
            pattern = jnp.where(column < boundary, patterns[0], patterns[1 + boundary % 2])
            masked = []
            for part in range(parts):
                rows = spectra_ref[pair, part].astype(jnp.float32)
                for at in range(0, fields, 2):
                    picked = jnp.where(row < 4, rows[at : at + 1], rows[at + 1 : at + 2])
                    masked.append(picked * pattern)
            masked = jnp.concatenate(masked, axis=0).astype(jnp.bfloat16)
            scratch[pair, :, 0:heights] = lax.dot_general(
                masked,
                legendre_ref[pair],
                (((1,), (1,)), ((), ())),
                preferred_element_type=jnp.float32,
            )
        return carry

    lax.fori_loop(0, steps, project, 0)
    blocks, _, lats, _ = out_ref.shape
    full, rest, per_slot, _ = packing(2 * scratch.shape[0], half)
    for sign in range(2):
        rows = []
        for coefficient in range(half):
            halves = []
            for part in range(2):
                picked = scratch[:, 4 * coefficient + 2 * part + sign, :]
                halves.append(jnp.transpose(picked)[:heights])
            rows.append(jnp.concatenate(halves, axis=1))
        slots = [
            rows[row][:, chunk * LANES : (chunk + 1) * LANES]
            for chunk in range(full)
            for row in range(half)
        ]
        if rest:
            for at in range(0, half, per_slot):
                pieces = [row[:, full * LANES :] for row in rows[at : at + per_slot]]
                spare = LANES - rest * len(pieces)
                if spare:
                    pieces.append(jnp.zeros((heights, spare), jnp.float32))
                slots.append(jnp.concatenate(pieces, axis=1))
        for slot, values in enumerate(slots):
            values = values.astype(jnp.bfloat16)
            for b in range(blocks // 2):
                target = b if sign == 0 else blocks - 1 - b
                out_ref[target, slot] = values[b * lats : (b + 1) * lats]


def legendre_step(spectra, legendre, pair_waves, blocks):
    pairs, parts, fields, padded = spectra.shape
    heights = legendre.shape[1]
    block = 8 if pairs % 8 == 0 else 4
    lats = 2 * heights // blocks
    slots = packing(2 * pairs, parts * fields)[3]
    result = (blocks, slots, lats, LANES)
    return pl.pallas_call(
        functools.partial(legendre_kernel, block),
        out_shape=jax.ShapeDtypeStruct(result, jnp.bfloat16),
        in_specs=[
            pl.BlockSpec(memory_space=pltpu.SMEM),
            pl.BlockSpec(memory_space=pl.ANY),
            pl.BlockSpec(memory_space=pl.ANY),
        ],
        out_specs=pl.BlockSpec(memory_space=pltpu.VMEM),
        scratch_shapes=[
            pltpu.VMEM((pairs, 4 * parts * fields, max(heights, LANES)), jnp.float32),
            pltpu.VMEM((3, 8, padded), jnp.float32),
            pltpu.VMEM(spectra.shape, spectra.dtype),
            pltpu.VMEM(legendre.shape, legendre.dtype),
            pltpu.SemaphoreType.DMA((2, pairs // block)),
        ],
        name="legendre",
    )(pair_waves, spectra, legendre)


def trig(wave, offset, length, inverse):
    product = wave * offset
    turns = (product - jnp.round(product * inverse) * length) * inverse
    square = turns * turns
    sine = jnp.float32(SIN_PI[-1])
    for term in SIN_PI[-2::-1]:
        sine = sine * square + term
    sine = sine * turns
    cosine = jnp.float32(COS_PI[-1])
    for term in COS_PI[-2::-1]:
        cosine = cosine * square + term
    double = sine + sine
    return 1.0 - double * sine, double * cosine


def gather_rows(arrived, fields_ref, groups, waves):
    blocks = arrived.shape[0]
    full, rest, per_slot, _ = packing(waves, groups)
    for g in range(groups):
        pieces = [
            arrived[w, chunk * groups + g].astype(jnp.float32)
            for w in range(blocks)
            for chunk in range(full)
        ]
        if rest:
            slot, at = full * groups + g // per_slot, g % per_slot * rest
            ends = [arrived[w, slot].astype(jnp.float32) for w in range(blocks)]
            pieces += [end[:, at : at + rest] for end in ends]
        fields_ref[:, g, :] = jnp.concatenate(pieces, axis=1)


def doubled_shift(cosine, sine):
    c, s = cosine[4:5], sine[4:5]
    c, s = 1.0 - 2.0 * s * s, 2.0 * s * c
    return cosine * c - sine * s, sine * c + cosine * s


def tables_of(wave, length, inverse, table_ref):
    row = lax.broadcasted_iota(jnp.int32, (8, 1), 0).astype(jnp.float32)
    fine_cos, fine_sin = trig(wave, row, length, inverse)
    fine_neg = -fine_cos
    for top in range(LANES // 64):
        if top == 0:
            coarse_cos, coarse_sin = trig(wave, 8 * row, length, inverse)
        else:
            coarse_cos, coarse_sin = doubled_shift(coarse_cos, coarse_sin)
        for pair in range(4):
            cosines, sines = [], []
            for a in (2 * pair, 2 * pair + 1):
                c, s = coarse_cos[a : a + 1], coarse_sin[a : a + 1]
                cosines.append(c * fine_cos - s * fine_sin)
                sines.append(s * fine_neg - c * fine_sin)
            at = 64 * top + 16 * pair
            table_ref[at : at + 16, 0:M] = jnp.concatenate(cosines, axis=0).astype(jnp.bfloat16)
            table_ref[at : at + 16, M : 2 * M] = jnp.concatenate(sines, axis=0).astype(jnp.bfloat16)


def synthesis(wave, count, columns, points, fields, table_ref, left_ref):
    length = count.astype(jnp.float32)
    inverse = 1.0 / length
    local = fields.shape[0] // 2
    rows = columns * local
    weight = jnp.where(wave == 0, 1.0, jnp.where(2 * wave < length, 2.0, 0.0))
    column = (lax.broadcasted_iota(jnp.int32, (rows, 1), 0) // local).astype(jnp.float32)
    cosine, sine = trig(wave, points * column, length, inverse)
    real = jnp.concatenate([fields[:local] * weight] * columns, axis=0)
    imag = jnp.concatenate([fields[local:] * weight] * columns, axis=0)
    real, imag = real * cosine - imag * sine, real * sine + imag * cosine
    row = lax.broadcasted_iota(jnp.int32, (8, 1), 0).astype(jnp.float32)
    for block in range(pl.cdiv(points, LANES)):
        if block == 0:
            block_cos, block_sin = trig(wave, LANES * row, length, inverse)
        elif block == 8:
            block_cos, block_sin = doubled_shift(block_cos, block_sin)
        elif block % 8 == 0:
            block_cos, block_sin = trig(wave, LANES * (block + row), length, inverse)
        c = block_cos[block % 8 : block % 8 + 1]
        s = block_sin[block % 8 : block % 8 + 1]
        at = block * rows
        left_ref[at : at + rows, 0:M] = (real * c - imag * s).astype(jnp.bfloat16)
        left_ref[at : at + rows, M : 2 * M] = (real * s + imag * c).astype(jnp.bfloat16)
    return lax.dot_general(
        left_ref[...],
        table_ref[...],
        (((1,), (1,)), ((), ())),
        preferred_element_type=jnp.float32,
    )


def slot_latitude(i, lats, blocks):
    return jnp.where(lax.axis_index("wa") >= blocks // 2, lats - 1 - i, i)


def fourier_kernel(
    groups, points, points_ref, pairs_ref, sent, landed,
    arrived, fields_ref, tables_ref, left_ref, sums_ref, leaving,
    own_sem, send_band, recv_band, send_level, recv_level,
):
    lats = tables_ref.shape[0]
    columns, parts = landed.shape[:2]
    blocks = arrived.shape[0]
    local = groups // 2
    me, level = lax.axis_index("wa"), lax.axis_index("vert")
    barrier = pltpu.get_barrier_semaphore()

    def greet_band(d, carry):
        pl.semaphore_signal(
            barrier, inc=1, device_id=(lax.rem(me + d, blocks), level), device_id_type=MESH
        )
        return carry

    def greet_level(e, carry):
        pl.semaphore_signal(
            barrier, inc=1, device_id=(me, lax.rem(level + e, columns)), device_id_type=MESH
        )
        return carry

    lax.fori_loop(1, blocks, greet_band, 0)
    lax.fori_loop(1, columns, greet_level, 0)
    own = pltpu.make_async_copy(sent.at[me], arrived.at[me], own_sem.at[0])
    own.start()

    def band_copy(d):
        target = lax.rem(me + d, blocks)
        return pltpu.make_async_remote_copy(
            src_ref=sent.at[target],
            dst_ref=arrived.at[me],
            send_sem=send_band.at[d],
            recv_sem=recv_band.at[d],
            device_id=(target, level),
            device_id_type=MESH,
        )

    def band_arrival(d):
        source = lax.rem(me + blocks - d, blocks)
        return pltpu.make_async_remote_copy(
            src_ref=sent.at[source],
            dst_ref=arrived.at[source],
            send_sem=send_band.at[d],
            recv_sem=recv_band.at[d],
            device_id=(source, level),
            device_id_type=MESH,
        )

    def level_copy(part, e):
        target = lax.rem(level + e, columns)
        return pltpu.make_async_remote_copy(
            src_ref=leaving.at[part, target],
            dst_ref=landed.at[level, part],
            send_sem=send_level.at[part, e],
            recv_sem=recv_level.at[part, e],
            device_id=(me, target),
            device_id_type=MESH,
        )

    def level_arrival(part, e):
        source = lax.rem(level + columns - e, columns)
        return pltpu.make_async_remote_copy(
            src_ref=leaving.at[part, source],
            dst_ref=landed.at[source, part],
            send_sem=send_level.at[part, e],
            recv_sem=recv_level.at[part, e],
            device_id=(me, source),
            device_id_type=MESH,
        )

    def start_band(d, carry):
        band_copy(d).start()
        return carry

    wave = packed_order(pairs_ref[...].astype(jnp.float32).reshape(1, -1), blocks)

    def make_tables(i, carry):
        length = points_ref[slot_latitude(i, lats, blocks)].astype(jnp.float32)
        tables_of(wave, length, 1.0 / length, tables_ref.at[i])
        return carry

    early = lats // 4
    lax.fori_loop(0, early, make_tables, 0)
    pl.semaphore_wait(barrier, blocks + columns - 2)
    lax.fori_loop(1, blocks, start_band, 0)
    lax.fori_loop(early, lats, make_tables, 0)
    own.wait()

    def finish_band(d, carry):
        band_arrival(d).wait_recv()
        band_copy(d).wait_send()
        return carry

    lax.fori_loop(1, blocks, finish_band, 0)
    gather_rows(arrived, fields_ref, groups, M // blocks)
    each = lats // parts
    rows = columns * local

    def one_part(part, carry):
        for j in range(each):
            i = part * each + j
            product = synthesis(
                wave,
                points_ref[slot_latitude(i, lats, blocks)],
                columns,
                points,
                fields_ref[i],
                tables_ref.at[i],
                left_ref,
            )
            for block in range(product.shape[0] // rows):
                for v in range(columns):
                    at = block * rows + v * local
                    sums_ref[v, j * local : (j + 1) * local, block * LANES : (block + 1) * LANES] = (
                        product[at : at + local]
                    )
        for v in range(columns):
            leaving[part, v] = sums_ref[v].astype(jnp.bfloat16)

        def start_level(e, inner):
            level_copy(part, e).start()
            return inner

        lax.fori_loop(1, columns, start_level, 0)
        pltpu.make_async_copy(
            leaving.at[part, level], landed.at[level, part], own_sem.at[1 + part]
        ).start()
        return carry

    lax.fori_loop(0, parts, one_part, 0)

    def finish_part(part, carry):
        def finish(e, inner):
            level_arrival(part, e).wait_recv()
            level_copy(part, e).wait_send()
            return inner

        pltpu.make_async_copy(
            leaving.at[part, level], landed.at[level, part], own_sem.at[1 + part]
        ).wait()
        return lax.fori_loop(1, columns, finish, carry)

    lax.fori_loop(0, parts, finish_part, 0)


def fourier_step(sent, pair_waves, points, points_device, groups, columns):
    blocks, slots, lats, _ = sent.shape
    local = groups // 2
    parts = 2
    chunks = pl.cdiv(points_device, LANES)
    rows = lats // parts * local
    return pl.pallas_call(
        functools.partial(fourier_kernel, groups, points_device),
        out_shape=jax.ShapeDtypeStruct((columns, parts, rows, chunks * LANES), jnp.bfloat16),
        in_specs=[
            pl.BlockSpec(memory_space=pltpu.SMEM),
            pl.BlockSpec(memory_space=pltpu.VMEM),
            pl.BlockSpec(memory_space=pl.ANY),
        ],
        out_specs=pl.BlockSpec(memory_space=pl.ANY),
        scratch_shapes=[
            pltpu.VMEM((blocks, slots, lats, LANES), jnp.bfloat16),
            pltpu.VMEM((lats, groups, M), jnp.float32),
            pltpu.VMEM((lats, LANES, 2 * M), jnp.bfloat16),
            pltpu.VMEM((chunks * columns * local, 2 * M), jnp.bfloat16),
            pltpu.VMEM((columns, rows, chunks * LANES), jnp.float32),
            pltpu.VMEM((parts, columns, rows, chunks * LANES), jnp.bfloat16),
            pltpu.SemaphoreType.DMA((1 + parts,)),
            pltpu.SemaphoreType.DMA((blocks,)),
            pltpu.SemaphoreType.DMA((blocks,)),
            pltpu.SemaphoreType.DMA((parts, columns)),
            pltpu.SemaphoreType.DMA((parts, columns)),
        ],
        compiler_params=pltpu.CompilerParams(collective_id=0, has_side_effects=True),
        name="fourier",
    )(points, pair_waves, sent)


def place_kernel(blocks, points_ref, landed, out_ref):
    lats, fields, points = out_ref.shape
    columns, parts = landed.shape[:2]
    each, local = lats // parts, fields // columns
    first_point = lax.axis_index("vert") * points
    for part in range(parts):
        values = [landed[v, part].astype(jnp.float32) for v in range(columns)]
        for j in range(each):
            lat = slot_latitude(part * each + j, lats, blocks)
            rows = jnp.concatenate([value[j * local : (j + 1) * local] for value in values], axis=0)
            index = first_point + lax.broadcasted_iota(jnp.int32, rows.shape, 1)
            out_ref[lat] = jnp.where(index < points_ref[lat], rows, 0.0)[:, :points]


def place_step(landed, points, points_device, lats, fields, blocks):
    return pl.pallas_call(
        functools.partial(place_kernel, blocks),
        out_shape=jax.ShapeDtypeStruct((lats, fields, points_device), jnp.float32),
        in_specs=[
            pl.BlockSpec(memory_space=pltpu.SMEM),
            pl.BlockSpec(memory_space=pltpu.VMEM),
        ],
        out_specs=pl.BlockSpec(memory_space=pltpu.VMEM),
        name="place",
    )(points, landed)


def body(spectra, legendre, pair_waves, points):
    blocks, columns = lax.axis_size("wa"), lax.axis_size("vert")
    step_length = 8 * columns
    points_device = 8 * ((4 * M + 16 + step_length - 1) // step_length)
    groups = spectra.shape[1] * spectra.shape[2]
    sent = legendre_step(spectra, jnp.swapaxes(legendre, 1, 2), pair_waves, blocks)
    landed = fourier_step(sent, pair_waves, points, points_device, groups, columns)
    fields = columns * groups // 2
    return place_step(landed, points, points_device, points.shape[0], fields, blocks)


def solution(mesh):
    in_specs = (P("wa", None, "vert", None), P("wa", None, None), P(), P("wa"))
    out_specs = P("wa", None, "vert")
    return jax.shard_map(body, mesh=mesh, in_specs=in_specs, out_specs=out_specs, check_vma=False)
```

```python
import functools

import jax
import jax.numpy as jnp
from jax import lax
from jax.experimental import pallas as pl
from jax.experimental.pallas import tpu as pltpu
from jax.sharding import PartitionSpec as P

M = 1280
LANES = 128
MESH = pl.DeviceIdType.MESH
SIN_PI = (3.141592640183955, -5.167710090327305, 2.5500776596396157, -0.5982921588969844, 0.07765940708214343)
COS_PI = (0.9999999534665123, -4.934792858655412, 4.058411913769657, -1.3318801587031317, 0.21969679350917085)


def packing(waves, groups):
    full, rest = divmod(waves, LANES)
    per_slot = LANES // rest if rest else 1
    slots = full * groups + (-(-groups // per_slot) if rest else 0)
    return full, rest, per_slot, slots


def packed_order(pairs, blocks):
    count = pairs.shape[1] // blocks
    cut = 2 * count // LANES * LANES
    waves = []
    for block in range(blocks):
        lower = pairs[:, block * count : (block + 1) * count]
        waves.append(jnp.concatenate([lower, M - 1 - lower], axis=1))
    heads = [wave[:, :cut] for wave in waves] if cut else []
    tails = [wave[:, cut:] for wave in waves] if cut < 2 * count else []
    return jnp.concatenate(heads + tails, axis=1)


def legendre_kernel(
    pair_block, waves_ref, spectra, legendre, out_ref,
    scratch, patterns, spectra_ref, legendre_ref, sems,
):
    parts, fields, padded = spectra_ref.shape[1:]
    half = parts * fields
    heights = legendre_ref.shape[1]
    num_pairs = scratch.shape[0]
    column = lax.broadcasted_iota(jnp.int32, (8, padded), 1)
    row = lax.broadcasted_iota(jnp.int32, (8, padded), 0)

    def copies(step):
        at = pl.ds(step * pair_block, pair_block)
        return (
            pltpu.make_async_copy(spectra.at[at], spectra_ref.at[at], sems.at[0, step]),
            pltpu.make_async_copy(legendre.at[at], legendre_ref.at[at], sems.at[1, step]),
        )

    def start(step, carry):
        for copy in copies(step):
            copy.start()
        return carry

    steps = num_pairs // pair_block
    lax.fori_loop(0, steps, start, 0)

    later = (row // 2) % 2 == 1
    signed = row % 2 == 1
    plain = jnp.where(signed & (column % 2 == 1), -1.0, 1.0)
    even = jnp.where(later & (column < M + 1), plain, 0.0)
    patterns[0] = jnp.where(later, 0.0, plain)
    patterns[1] = even
    patterns[2] = jnp.where(signed, -even, even)

    def project(step, carry):
        for copy in copies(step):
            copy.wait()
        for i in range(pair_block):
            pair = step * pair_block + i
            boundary = M - waves_ref[lax.axis_index("wa") * num_pairs + pair]
            pattern = jnp.where(column < boundary, patterns[0], patterns[1 + boundary % 2])
            masked = []
            for part in range(parts):
                rows = spectra_ref[pair, part].astype(jnp.float32)
                for at in range(0, fields, 2):
                    picked = jnp.where(row < 4, rows[at : at + 1], rows[at + 1 : at + 2])
                    masked.append(picked * pattern)
            masked = jnp.concatenate(masked, axis=0).astype(jnp.bfloat16)
            scratch[pair, :, 0:heights] = lax.dot_general(
                masked,
                legendre_ref[pair],
                (((1,), (1,)), ((), ())),
                preferred_element_type=jnp.float32,
            )
        return carry

    lax.fori_loop(0, steps, project, 0)
    blocks, _, lats, _ = out_ref.shape
    full, rest, per_slot, _ = packing(2 * scratch.shape[0], half)
    for sign in range(2):
        rows = []
        for coefficient in range(half):
            halves = []
            for part in range(2):
                picked = scratch[:, 4 * coefficient + 2 * part + sign, :]
                halves.append(jnp.transpose(picked)[:heights])
            rows.append(jnp.concatenate(halves, axis=1))
        slots = [
            rows[row][:, chunk * LANES : (chunk + 1) * LANES]
            for chunk in range(full)
            for row in range(half)
        ]
        if rest:
            for at in range(0, half, per_slot):
                pieces = [row[:, full * LANES :] for row in rows[at : at + per_slot]]
                spare = LANES - rest * len(pieces)
                if spare:
                    pieces.append(jnp.zeros((heights, spare), jnp.float32))
                slots.append(jnp.concatenate(pieces, axis=1))
        for slot, values in enumerate(slots):
            values = values.astype(jnp.bfloat16)
            for b in range(blocks // 2):
                target = b if sign == 0 else blocks - 1 - b
                out_ref[target, slot] = values[b * lats : (b + 1) * lats]


def legendre_step(spectra, legendre, pair_waves, blocks):
    pairs, parts, fields, padded = spectra.shape
    heights = legendre.shape[1]
    block = 8 if pairs % 8 == 0 else 4
    lats = 2 * heights // blocks
    slots = packing(2 * pairs, parts * fields)[3]
    result = (blocks, slots, lats, LANES)
    return pl.pallas_call(
        functools.partial(legendre_kernel, block),
        out_shape=jax.ShapeDtypeStruct(result, jnp.bfloat16),
        in_specs=[
            pl.BlockSpec(memory_space=pltpu.SMEM),
            pl.BlockSpec(memory_space=pl.ANY),
            pl.BlockSpec(memory_space=pl.ANY),
        ],
        out_specs=pl.BlockSpec(memory_space=pltpu.VMEM),
        scratch_shapes=[
            pltpu.VMEM((pairs, 4 * parts * fields, max(heights, LANES)), jnp.float32),
            pltpu.VMEM((3, 8, padded), jnp.float32),
            pltpu.VMEM(spectra.shape, spectra.dtype),
            pltpu.VMEM(legendre.shape, legendre.dtype),
            pltpu.SemaphoreType.DMA((2, pairs // block)),
        ],
        name="legendre",
    )(pair_waves, spectra, legendre)


def trig(wave, offset, length, inverse):
    product = wave * offset
    turns = (product - jnp.round(product * inverse) * length) * inverse
    square = turns * turns
    sine = jnp.float32(SIN_PI[-1])
    for term in SIN_PI[-2::-1]:
        sine = sine * square + term
    sine = sine * turns
    cosine = jnp.float32(COS_PI[-1])
    for term in COS_PI[-2::-1]:
        cosine = cosine * square + term
    double = sine + sine
    return 1.0 - double * sine, double * cosine


def gather_rows(arrived, fields_ref, groups, waves):
    blocks = arrived.shape[0]
    full, rest, per_slot, _ = packing(waves, groups)
    for g in range(groups):
        pieces = [
            arrived[w, chunk * groups + g].astype(jnp.float32)
            for w in range(blocks)
            for chunk in range(full)
        ]
        if rest:
            slot, at = full * groups + g // per_slot, g % per_slot * rest
            ends = [arrived[w, slot].astype(jnp.float32) for w in range(blocks)]
            pieces += [end[:, at : at + rest] for end in ends]
        fields_ref[:, g, :] = jnp.concatenate(pieces, axis=1)


def doubled_shift(cosine, sine):
    c, s = cosine[4:5], sine[4:5]
    c, s = 1.0 - 2.0 * s * s, 2.0 * s * c
    return cosine * c - sine * s, sine * c + cosine * s


def tables_of(wave, length, inverse, table_ref, turns_ref):
    row = lax.broadcasted_iota(jnp.int32, (8, 1), 0).astype(jnp.float32)
    fine_cos, fine_sin = trig(wave, row, length, inverse)
    fine_neg = -fine_cos
    for top in range(LANES // 64):
        if top == 0:
            coarse_cos, coarse_sin = trig(wave, 8 * row, length, inverse)
        else:
            coarse_cos, coarse_sin = doubled_shift(coarse_cos, coarse_sin)
        turns_ref[0, 8 * top : 8 * top + 8] = coarse_cos
        turns_ref[1, 8 * top : 8 * top + 8] = coarse_sin
        for pair in range(4):
            cosines, sines = [], []
            for a in (2 * pair, 2 * pair + 1):
                c = turns_ref[0, pl.ds(8 * top + a, 8, stride=0), :]
                s = turns_ref[1, pl.ds(8 * top + a, 8, stride=0), :]
                cosines.append(c * fine_cos - s * fine_sin)
                sines.append(s * fine_neg - c * fine_sin)
            at = 64 * top + 16 * pair
            table_ref[at : at + 16, 0:M] = jnp.concatenate(cosines, axis=0).astype(jnp.bfloat16)
            table_ref[at : at + 16, M : 2 * M] = jnp.concatenate(sines, axis=0).astype(jnp.bfloat16)


def synthesis(wave, count, columns, points, fields, table_ref, left_ref):
    length = count.astype(jnp.float32)
    inverse = 1.0 / length
    local = fields.shape[0] // 2
    rows = columns * local
    weight = jnp.where(wave == 0, 1.0, jnp.where(2 * wave < length, 2.0, 0.0))
    column = (lax.broadcasted_iota(jnp.int32, (rows, 1), 0) // local).astype(jnp.float32)
    cosine, sine = trig(wave, points * column, length, inverse)
    real = jnp.concatenate([fields[:local] * weight] * columns, axis=0)
    imag = jnp.concatenate([fields[local:] * weight] * columns, axis=0)
    real, imag = real * cosine - imag * sine, real * sine + imag * cosine
    row = lax.broadcasted_iota(jnp.int32, (8, 1), 0).astype(jnp.float32)
    for block in range(pl.cdiv(points, LANES)):
        if block == 0:
            block_cos, block_sin = trig(wave, LANES * row, length, inverse)
        elif block == 8:
            block_cos, block_sin = doubled_shift(block_cos, block_sin)
        elif block % 8 == 0:
            block_cos, block_sin = trig(wave, LANES * (block + row), length, inverse)
        c = block_cos[block % 8 : block % 8 + 1]
        s = block_sin[block % 8 : block % 8 + 1]
        at = block * rows
        left_ref[at : at + rows, 0:M] = (real * c - imag * s).astype(jnp.bfloat16)
        left_ref[at : at + rows, M : 2 * M] = (real * s + imag * c).astype(jnp.bfloat16)
    return lax.dot_general(
        left_ref[...],
        table_ref[...],
        (((1,), (1,)), ((), ())),
        preferred_element_type=jnp.float32,
    )


def slot_latitude(i, lats, blocks):
    return jnp.where(lax.axis_index("wa") >= blocks // 2, lats - 1 - i, i)


def fourier_kernel(
    groups, points, points_ref, pairs_ref, sent, landed,
    arrived, fields_ref, tables_ref, turns_ref, left_ref, sums_ref, leaving,
    own_sem, send_band, recv_band, send_level, recv_level,
):
    lats = tables_ref.shape[0]
    columns, parts = landed.shape[:2]
    blocks = arrived.shape[0]
    local = groups // 2
    me, level = lax.axis_index("wa"), lax.axis_index("vert")
    barrier = pltpu.get_barrier_semaphore()

    def greet_band(d, carry):
        pl.semaphore_signal(
            barrier, inc=1, device_id=(lax.rem(me + d, blocks), level), device_id_type=MESH
        )
        return carry

    def greet_level(e, carry):
        pl.semaphore_signal(
            barrier, inc=1, device_id=(me, lax.rem(level + e, columns)), device_id_type=MESH
        )
        return carry

    lax.fori_loop(1, blocks, greet_band, 0)
    lax.fori_loop(1, columns, greet_level, 0)
    own = pltpu.make_async_copy(sent.at[me], arrived.at[me], own_sem.at[0])
    own.start()

    def band_copy(d):
        target = lax.rem(me + d, blocks)
        return pltpu.make_async_remote_copy(
            src_ref=sent.at[target],
            dst_ref=arrived.at[me],
            send_sem=send_band.at[d],
            recv_sem=recv_band.at[d],
            device_id=(target, level),
            device_id_type=MESH,
        )

    def band_arrival(d):
        source = lax.rem(me + blocks - d, blocks)
        return pltpu.make_async_remote_copy(
            src_ref=sent.at[source],
            dst_ref=arrived.at[source],
            send_sem=send_band.at[d],
            recv_sem=recv_band.at[d],
            device_id=(source, level),
            device_id_type=MESH,
        )

    def level_copy(part, e):
        target = lax.rem(level + e, columns)
        return pltpu.make_async_remote_copy(
            src_ref=leaving.at[part, target],
            dst_ref=landed.at[level, part],
            send_sem=send_level.at[part, e],
            recv_sem=recv_level.at[part, e],
            device_id=(me, target),
            device_id_type=MESH,
        )

    def level_arrival(part, e):
        source = lax.rem(level + columns - e, columns)
        return pltpu.make_async_remote_copy(
            src_ref=leaving.at[part, source],
            dst_ref=landed.at[source, part],
            send_sem=send_level.at[part, e],
            recv_sem=recv_level.at[part, e],
            device_id=(me, source),
            device_id_type=MESH,
        )

    def start_band(d, carry):
        band_copy(d).start()
        return carry

    wave = packed_order(pairs_ref[...].astype(jnp.float32).reshape(1, -1), blocks)

    def make_tables(i, carry):
        length = points_ref[slot_latitude(i, lats, blocks)].astype(jnp.float32)
        tables_of(wave, length, 1.0 / length, tables_ref.at[i], turns_ref)
        return carry

    early = lats // 4
    lax.fori_loop(0, early, make_tables, 0)
    pl.semaphore_wait(barrier, blocks + columns - 2)
    lax.fori_loop(1, blocks, start_band, 0)
    lax.fori_loop(early, lats, make_tables, 0)
    own.wait()

    def finish_band(d, carry):
        band_arrival(d).wait_recv()
        band_copy(d).wait_send()
        return carry

    lax.fori_loop(1, blocks, finish_band, 0)
    gather_rows(arrived, fields_ref, groups, M // blocks)
    each = lats // parts
    rows = columns * local

    def one_part(part, carry):
        for j in range(each):
            i = part * each + j
            product = synthesis(
                wave,
                points_ref[slot_latitude(i, lats, blocks)],
                columns,
                points,
                fields_ref[i],
                tables_ref.at[i],
                left_ref,
            )
            for block in range(product.shape[0] // rows):
                for v in range(columns):
                    at = block * rows + v * local
                    sums_ref[v, j * local : (j + 1) * local, block * LANES : (block + 1) * LANES] = (
                        product[at : at + local]
                    )
        for v in range(columns):
            leaving[part, v] = sums_ref[v].astype(jnp.bfloat16)

        def start_level(e, inner):
            level_copy(part, e).start()
            return inner

        lax.fori_loop(1, columns, start_level, 0)
        pltpu.make_async_copy(
            leaving.at[part, level], landed.at[level, part], own_sem.at[1 + part]
        ).start()
        return carry

    lax.fori_loop(0, parts, one_part, 0)

    def finish_part(part, carry):
        def finish(e, inner):
            level_arrival(part, e).wait_recv()
            level_copy(part, e).wait_send()
            return inner

        pltpu.make_async_copy(
            leaving.at[part, level], landed.at[level, part], own_sem.at[1 + part]
        ).wait()
        return lax.fori_loop(1, columns, finish, carry)

    lax.fori_loop(0, parts, finish_part, 0)


def fourier_step(sent, pair_waves, points, points_device, groups, columns):
    blocks, slots, lats, _ = sent.shape
    local = groups // 2
    parts = 2
    chunks = pl.cdiv(points_device, LANES)
    rows = lats // parts * local
    return pl.pallas_call(
        functools.partial(fourier_kernel, groups, points_device),
        out_shape=jax.ShapeDtypeStruct((columns, parts, rows, chunks * LANES), jnp.bfloat16),
        in_specs=[
            pl.BlockSpec(memory_space=pltpu.SMEM),
            pl.BlockSpec(memory_space=pltpu.VMEM),
            pl.BlockSpec(memory_space=pl.ANY),
        ],
        out_specs=pl.BlockSpec(memory_space=pl.ANY),
        scratch_shapes=[
            pltpu.VMEM((blocks, slots, lats, LANES), jnp.bfloat16),
            pltpu.VMEM((lats, groups, M), jnp.float32),
            pltpu.VMEM((lats, LANES, 2 * M), jnp.bfloat16),
            pltpu.VMEM((2, LANES // 8, M), jnp.float32),
            pltpu.VMEM((chunks * columns * local, 2 * M), jnp.bfloat16),
            pltpu.VMEM((columns, rows, chunks * LANES), jnp.float32),
            pltpu.VMEM((parts, columns, rows, chunks * LANES), jnp.bfloat16),
            pltpu.SemaphoreType.DMA((1 + parts,)),
            pltpu.SemaphoreType.DMA((blocks,)),
            pltpu.SemaphoreType.DMA((blocks,)),
            pltpu.SemaphoreType.DMA((parts, columns)),
            pltpu.SemaphoreType.DMA((parts, columns)),
        ],
        compiler_params=pltpu.CompilerParams(collective_id=0, has_side_effects=True),
        name="fourier",
    )(points, pair_waves, sent)


def place_kernel(blocks, points_ref, landed, out_ref):
    lats, fields, points = out_ref.shape
    columns, parts = landed.shape[:2]
    each, local = lats // parts, fields // columns
    first_point = lax.axis_index("vert") * points
    for part in range(parts):
        values = [landed[v, part].astype(jnp.float32) for v in range(columns)]
        for j in range(each):
            lat = slot_latitude(part * each + j, lats, blocks)
            rows = jnp.concatenate([value[j * local : (j + 1) * local] for value in values], axis=0)
            index = first_point + lax.broadcasted_iota(jnp.int32, rows.shape, 1)
            out_ref[lat] = jnp.where(index < points_ref[lat], rows, 0.0)[:, :points]


def place_step(landed, points, points_device, lats, fields, blocks):
    return pl.pallas_call(
        functools.partial(place_kernel, blocks),
        out_shape=jax.ShapeDtypeStruct((lats, fields, points_device), jnp.float32),
        in_specs=[
            pl.BlockSpec(memory_space=pltpu.SMEM),
            pl.BlockSpec(memory_space=pltpu.VMEM),
        ],
        out_specs=pl.BlockSpec(memory_space=pltpu.VMEM),
        name="place",
    )(points, landed)


def body(spectra, legendre, pair_waves, points):
    blocks, columns = lax.axis_size("wa"), lax.axis_size("vert")
    step_length = 8 * columns
    points_device = 8 * ((4 * M + 16 + step_length - 1) // step_length)
    groups = spectra.shape[1] * spectra.shape[2]
    sent = legendre_step(spectra, jnp.swapaxes(legendre, 1, 2), pair_waves, blocks)
    landed = fourier_step(sent, pair_waves, points, points_device, groups, columns)
    fields = columns * groups // 2
    return place_step(landed, points, points_device, points.shape[0], fields, blocks)


def solution(mesh):
    in_specs = (P("wa", None, "vert", None), P("wa", None, None), P(), P("wa"))
    out_specs = P("wa", None, "vert")
    return jax.shard_map(body, mesh=mesh, in_specs=in_specs, out_specs=out_specs, check_vma=False)
```
